128 devices in a mesh: gx: 16 (over z, x), gy: 4 (over y_lo, core), gz: 2 (over y_hi).
Axes of the slice: x: 4, y: 4 (y_hi: 2, y_lo: 2; y = y_hi * 2 + y_lo), z: 4, core: 2. Of those that a mesh axis runs over, the one named last changes fastest.
Arguments:
- adjoint_efield: float32 [3, 48, 128, 2048], P(None, 'gz', 'gx', 'gy'), may hold values from -6 to 6
- adjoint_hfield: float32 [3, 48, 128, 2048], P(None, 'gz', 'gx', 'gy'), may hold values from -6 to 6
- forward_efield: float32 [3, 48, 128, 2048], P(None, 'gz', 'gx', 'gy'), may hold values from -6 to 6
- material: int32 [48, 128, 2048], P('gz', 'gx', 'gy'), may hold values from 0 to 3
- permittivity: float32 [4], replicated, may hold values from 1 to 12
- design_mask: int32 [16, 256], P('gx', 'gy'), may hold values 0 or 1
- grad_sum: float32 [32, 128, 2048], P('gz', 'gx', 'gy'), may hold values from -6 to 6
Outputs:
- efield_next: float32 [3, 48, 128, 2048], P(None, 'gz', 'gx', 'gy')
- hfield_next: float32 [3, 48, 128, 2048], P(None, 'gz', 'gx', 'gy')
- grad_total: float32 [32, 128, 2048], P('gz', 'gx', 'gy')
- grad_filtered: float32 [32, 128, 2048], P('gz', 'gx', 'gy')
The draws below stay inside these ranges and needn't reach their ends.
Inputs may be any that keep to these rules, and one draw needn't show every extreme that they name: material indices name rows of permittivity.
All inputs are finite; a program needn't handle non-finite values. No bound on the sum of `design_mask` on one device may be relied on, other than what follows from the above.
Results may differ from the reference program's by a relative error of at most 0.0003.
Values sent between devices are 32-bit elements; how exact they have to be, the bound alone decides.
A program may use at most 128 MiB of HBM per device.

```python
import math
import jax
import jax.numpy as jnp
from jax import lax

CZ = 24
LAY_DEV = 16
RADIUS = 6
BLOCK = 8
MATS = 4
NX = 128
NY = 2048
NZ = 48
LAYERS = 32


def touch_ends(entries, key, smallest, high):
    index_at = [jax.random.randint(jax.random.fold_in(key, axis), (), 0, length) for axis, length in enumerate(entries.shape)]
    widest = entries.shape.index(max(entries.shape))
    neighbour = index_at[:widest] + [(index_at[widest] + 1) % entries.shape[widest]] + index_at[widest + 1:]
    return entries.at[tuple(index_at)].set(smallest).at[tuple(neighbour)].set(high)


def block_scale(rng, shape, cuts, low, high):
    loudness = 1.0
    for axis_at, blocks in cuts:
        heights = jax.random.uniform(jax.random.fold_in(jax.random.fold_in(rng, 6), axis_at), (blocks,), jnp.float32, low / len(cuts), high / len(cuts))
        loudness = loudness * jnp.repeat(jnp.exp(heights), shape[axis_at] // blocks).reshape((-1,) + (1,) * (len(shape) - 1 - axis_at))
    return loudness


def scatter_about(rng, dims, scale, limit, shards=(), kind=jnp.bfloat16):
    result = scale * jax.random.normal(rng, dims, jnp.float32)
    if shards:
        result = result * block_scale(rng, dims, shards, -0.22, 0.18)
    return jnp.clip(result, -limit, limit).astype(kind)


def setup_inputs(seed: int = 0) -> dict:
    streams_of = jax.random.split(jax.random.key(seed), 8)
    adjoint_efield = scatter_about(streams_of[0], (3, NZ, NX, NY), 1.0, 6.0, ((1, 2), (2, 16), (3, 4)), jnp.float32)
    adjoint_hfield = scatter_about(streams_of[1], (3, NZ, NX, NY), 1.0, 6.0, ((1, 2), (2, 16), (3, 4)), jnp.float32)
    forward_efield = scatter_about(streams_of[2], (3, NZ, NX, NY), 1.0, 6.0, ((1, 2), (2, 16), (3, 4)), jnp.float32)
    material = touch_ends(jax.random.randint(streams_of[3], (NZ, NX, NY), 0, MATS), jax.random.fold_in(streams_of[3], 1), 0, MATS - 1).astype(jnp.int32)
    permittivity = jnp.clip(jnp.exp(jax.random.uniform(streams_of[4], (MATS,), jnp.float32, math.log(1.0), math.log(12.0))), 1.0, 12.0)
    design_mask = touch_ends((jax.random.randint(streams_of[5], (NX // BLOCK, NY // BLOCK), 0, 2) < 1).astype(jnp.int32), jax.random.fold_in(streams_of[5], 1), 0, 1)
    grad_sum = scatter_about(streams_of[6], (LAYERS, NX, NY), 1.0, 6.0, ((0, 2), (1, 16), (2, 4)), jnp.float32)
    return dict(adjoint_efield=adjoint_efield, adjoint_hfield=adjoint_hfield, forward_efield=forward_efield, material=material, permittivity=permittivity, design_mask=design_mask, grad_sum=grad_sum)


COURANT = 0.5

def curl(parts, differ):
    return (differ(parts[2], 2) - differ(parts[1], 0), differ(parts[0], 0) - differ(parts[2], 1), differ(parts[1], 1) - differ(parts[0], 2))

def advance(extended, inv_permit):
    inner_shape = (extended.shape[1] - 2, extended.shape[2] - 2, extended.shape[3] - 2)
    outer_shape = tuple((count + 1 for count in inner_shape))

    def forward(field, direction):
        unit_step = tuple((1 if which == direction else 0 for which in range(3)))
        upper_part = lax.slice(field, unit_step, tuple((a + b for a, b in zip(unit_step, outer_shape))))
        return upper_part - lax.slice(field, (0, 0, 0), outer_shape)

    def backward(field, direction):
        lower_start = tuple((0 if which == direction else 1 for which in range(3)))
        centre_part = lax.slice(field, (1, 1, 1), tuple((1 + count for count in inner_shape)))
        return centre_part - lax.slice(field, lower_start, tuple((a + b for a, b in zip(lower_start, inner_shape))))
    efield_old = [extended[component] for component in range(3)]
    curl_e = curl(efield_old, forward)
    h_new = [lax.slice(extended[3 + component], (0, 0, 0), outer_shape) - COURANT * curl_e[component] for component in range(3)]
    curl_h = curl(h_new, backward)
    inner_end = tuple((1 + count for count in inner_shape))
    e_next = [lax.slice(efield_old[component], (1, 1, 1), inner_end) + COURANT * inv_permit * curl_h[component] for component in range(3)]
    h_next = [lax.slice(h_new[component], (1, 1, 1), inner_end) for component in range(3)]
    return (jnp.stack(e_next), jnp.stack(h_next))

def inverse_permittivity(material, permittivity):
    permit = jnp.zeros(material.shape, jnp.float32)
    for which in range(permittivity.shape[0]):
        permit = permit + jnp.where(material == which, permittivity[which], jnp.float32(0.0))
    return 1.0 / permit

def expand_mask(design_mask):
    return jnp.repeat(jnp.repeat(design_mask, BLOCK, 0), BLOCK, 1).astype(jnp.float32)

def cone_weight(offset_x, offset_y, radius):
    distance = jnp.sqrt(offset_x * offset_x + offset_y * offset_y)
    return jnp.maximum(jnp.float32(radius) - distance, jnp.float32(0.0))

def cone_total(radius):
    span_values = jnp.arange(2 * radius + 1, dtype=jnp.float32) - radius
    return jnp.sum(cone_weight(span_values[:, None], span_values[None, :], radius))

def reference(adjoint_efield, adjoint_hfield, forward_efield, material, permittivity, design_mask, grad_sum):
    stacked = jnp.concatenate([adjoint_efield, adjoint_hfield], axis=0)
    extended = jnp.pad(stacked, ((0, 0), (1, 1), (1, 1), (1, 1)))
    efield_next, hfield_next = advance(extended, inverse_permittivity(material, permittivity))
    slab_first = CZ - LAY_DEV
    design_e = efield_next[:, slab_first:slab_first + LAYERS]
    design_f = forward_efield[:, slab_first:slab_first + LAYERS]
    grad_total = grad_sum + expand_mask(design_mask)[None] * lax.optimization_barrier(jnp.sum(design_f * design_e, axis=0))
    symmetric = grad_total + jnp.flip(grad_total, 1)
    padded = jnp.pad(symmetric, ((0, 0), (RADIUS, RADIUS), (RADIUS, RADIUS)))
    weight_sum = cone_total(RADIUS)
    filtered = jnp.zeros(symmetric.shape, jnp.float32)
    for shift_x in range(2 * RADIUS + 1):
        for shift_y in range(2 * RADIUS + 1):
            weight = cone_weight(jnp.float32(shift_x - RADIUS), jnp.float32(shift_y - RADIUS), RADIUS) / weight_sum
            filtered = filtered + weight * padded[:, shift_x:shift_x + NX, shift_y:shift_y + NY]
    return (efield_next, hfield_next, grad_total, filtered)
```

```python
import functools

import jax
import jax.numpy as jnp
import numpy as np
from jax import lax
from jax.experimental import pallas as pl
from jax.experimental.pallas import tpu as pltpu
from jax.sharding import PartitionSpec as P

RADIUS = 6
BLOCK = 8
COURANT = 0.5
MESH = pl.DeviceIdType.MESH
F32 = jnp.float32
ZC = 8
PADL = 128


def cone_table():
    span = np.arange(2 * RADIUS + 1, dtype=np.float32) - np.float32(RADIUS)
    dist = np.sqrt(span[:, None] ** 2 + span[None, :] ** 2).astype(np.float32)
    cone = np.maximum(np.float32(RADIUS) - dist, np.float32(0.0))
    return (cone / cone.sum(dtype=np.float32)).astype(np.float32)


def kernel(
    sizes,
    e_hbm, h_hbm, f_hbm, m_hbm, perm_ref, mask_ref, gs_hbm,
    eo_hbm, ho_hbm, gto_hbm, gfo_hbm,
    ev, hv, fv, mv, gsv, hn, en, gt, gf,
    xu_s, xu_r, xl_s, xl_r, yu_s, yu_r, yl_s, yl_r, zu_r, zl_r,
    gsend, gmir, wide, el_s, er_s, el_r, er_r,
    in_sem, out_sem,
    xu_ss, xu_rs, xl_ss, xl_rs, yu_ss, yu_rs, yl_ss, yl_rs, z_ss, z_rs,
    m_ss, m_rs, wp_ss, wp_rs, wm_ss, wm_rs, el_ss, el_rs, er_ss, er_rs,
):
    ngx, ngy = sizes
    gx, gy, gz = lax.axis_index("gx"), lax.axis_index("gy"), lax.axis_index("gz")
    ny = hv.shape[-1]
    nchunk = m_hbm.shape[0] // (8 * ZC)
    rows = nchunk * ZC * 8
    half = ny // 2

    def dev(dx=0, dy=0):
        return {
            "gx": lax.rem(gx + (dx + ngx), ngx),
            "gy": lax.rem(gy + (dy + ngy), ngy),
            "gz": gz,
        }

    mirror = {"gx": ngx - 1 - gx, "gy": gy, "gz": gz}
    zother = {"gx": gx, "gy": gy, "gz": 1 - gz}

    def load(i, src, dst):
        c = pltpu.make_async_copy(src, dst, in_sem.at[i])
        c.start()
        return c

    tiles = ny // PADL

    def lanes(t):
        return slice(t * PADL, (t + 1) * PADL)

    def plane(ref, *at):
        lead, r = at[:-1], at[-1]
        return jnp.concatenate(
            [ref[(*lead, t, pl.ds(r, 8), slice(None))] for t in range(tiles)], 1
        )

    def put(ref, value, *at):
        lead, r = at[:-1], at[-1]
        for t in range(tiles):
            ref[(*lead, t, pl.ds(r, 8), slice(None))] = value[:, lanes(t)]

    def strided(ref, *at):
        lead, r = at[:-1], at[-1]
        return jnp.concatenate(
            [ref[(*lead, t, pl.ds(r, 8, stride=8), slice(None))] for t in range(tiles)], 1
        )

    c_e = [load(t, e_hbm.at[:, :, lanes(t)], ev.at[:, t, 0:rows, :]) for t in range(tiles)]
    c_h = load(tiles, h_hbm, hv)
    c_m = load(tiles + 1, m_hbm, mv)
    c_f = load(tiles + 2, f_hbm, fv)
    c_g = load(tiles + 3, gs_hbm, gsv)

    barrier = pltpu.get_barrier_semaphore()
    peers = [dev(dx, dy) for dx in (-1, 0, 1) for dy in (-1, 0, 1) if (dx, dy) != (0, 0)]
    peers += [mirror, zother]
    for peer in peers:
        pl.semaphore_signal(barrier, inc=1, device_id=peer, device_id_type=MESH)

    sub = lax.broadcasted_iota(jnp.int32, (8, ny), 0)
    lane = lax.broadcasted_iota(jnp.int32, (8, PADL), 1)
    zero_tile = jnp.zeros((8, PADL), F32)

    low = gz == 0
    zcs = [jnp.where(low, nchunk - 1 - k, k) for k in range(nchunk)]

    def rows_at(z):
        return pl.multiple_of(z * 8, 8)

    nblk = mask_ref.shape[1]
    spread = (
        lax.broadcasted_iota(jnp.int32, (nblk, ny), 1) // BLOCK
        == lax.broadcasted_iota(jnp.int32, (nblk, ny), 0)
    ).astype(F32)
    mask = jnp.dot(
        jnp.broadcast_to(mask_ref[...].astype(F32), (8, nblk)), spread, preferred_element_type=F32
    )
    inv = [1.0 / jnp.full((8, ny), perm_ref[i], F32) for i in range(perm_ref.shape[0])]

    def rcopy(src, dst, ss, rs, peer):
        return pltpu.make_async_remote_copy(
            src_ref=src, dst_ref=dst, send_sem=ss, recv_sem=rs, device_id=peer, device_id_type=MESH
        )

    sends = []
    for c in c_e:
        c.wait()
    xu, yu = [], []
    for k in range(nchunk):
        z0 = zcs[k] * ZC
        for i, c in enumerate((1, 2)):
            xu_s[k, i] = strided(ev, c, rows_at(z0))
        acc = zero_tile
        for j in range(ZC):
            r = rows_at(z0 + j)
            for i, c in enumerate((0, 2)):
                tile = ev[c, 0, pl.ds(r, 8), :]
                at = 32 * i + j
                acc = jnp.where(lane == at, pltpu.roll(tile, at, 1) if at else tile, acc)
        yu_s[k] = acc
    pl.semaphore_wait(barrier, len(peers))
    zu = rcopy(ev.at[0:2, :, 0:8, :], zu_r, z_ss.at[0], z_rs.at[0], zother)
    pl.when(jnp.logical_not(low))(zu.start)
    for k in range(nchunk):
        c = rcopy(yu_s.at[k], yu_r.at[k], yu_ss.at[k], yu_rs.at[k], dev(0, -1))
        c.start()
        yu.append(c)
        c = rcopy(xu_s.at[k], xu_r.at[k], xu_ss.at[k], xu_rs.at[k], dev(-1, 0))
        c.start()
        xu.append(c)
    sends += yu + xu

    c_h.wait()

    @pl.when(low)
    def _():
        zu.wait_recv()
        ev[0:2, :, rows : rows + 8, :] = zu_r[...]

    @pl.when(jnp.logical_not(low))
    def _():
        ev[0:2, :, rows : rows + 8, :] = jnp.zeros((2, tiles, 8, PADL), F32)

    xl, yl, outs = [], [], []
    zl = None
    for k in range(nchunk):
        z0 = zcs[k] * ZC
        yu[k].wait_recv()
        xu[k].wait_recv()
        ytile = jnp.where(gy == ngy - 1, 0.0, yu_r[k])
        xu_r[k] = jnp.where(gx == ngx - 1, 0.0, xu_r[k])
        acc = zero_tile
        for j in range(ZC):
            r = rows_at(z0 + j)
            ex, ey, ez = (plane(ev, c, r) for c in range(3))
            exz, eyz = (plane(ev, c, r + 8) for c in range(2))
            hx, hy, hz = (hv[c, pl.ds(r, 8), :] for c in range(3))

            def above_y(f, at):
                tile = pltpu.roll(ytile, (PADL - at) % PADL, 1) if at else ytile
                return pltpu.roll(jnp.concatenate([f, tile], 1), ny + PADL - 1, 1)[:, :ny]

            def above_x(f, i):
                row = jnp.broadcast_to(xu_r[k, i, j : j + 1, :], (8, ny))
                return jnp.where(sub == 7, row, pltpu.roll(f, 7, 0))

            exy, ezy = above_y(ex, j), above_y(ez, 32 + j)
            eyx, ezx = above_x(ey, 0), above_x(ez, 1)
            hxn = hx - COURANT * ((ezy - ez) - (eyz - ey))
            hyn = hy - COURANT * ((exz - ex) - (ezx - ez))
            hzn = hz - COURANT * ((eyx - ey) - (exy - ex))
            for c, h in enumerate((hxn, hyn, hzn)):
                put(hn, h, c, r + 8)
            for i, h in enumerate((hzn, hxn)):
                at = 32 * i + j
                rolled = pltpu.roll(h[:, ny - PADL :], at + 1, 1)
                acc = jnp.where(lane == at, rolled, acc)
        yl_s[k] = acc
        for i, c in enumerate((1, 2)):
            xl_s[k, i] = strided(hn, c, rows_at(z0 + 1) + 7)
        if k == 0:
            zl = rcopy(hn.at[0:2, :, rows : rows + 8, :], zl_r, z_ss.at[1], z_rs.at[1], zother)
        c = rcopy(yl_s.at[k], yl_r.at[k], yl_ss.at[k], yl_rs.at[k], dev(0, 1))
        c.start()
        yl.append(c)
        c = rcopy(xl_s.at[k], xl_r.at[k], xl_ss.at[k], xl_rs.at[k], dev(1, 0))
        c.start()
        xl.append(c)
        if k == 0:
            pl.when(low)(zl.start)

    sends += yl + xl
    def store(src, dst):
        c = pltpu.make_async_copy(src, dst, out_sem.at[len(outs)])
        c.start()
        outs.append(c)

    for t in range(tiles):
        store(hn.at[:, t, 8 : rows + 8, :], ho_hbm.at[:, :, lanes(t)])

    c_m.wait()
    c_f.wait()
    c_g.wait()

    @pl.when(low)
    def _():
        hn[0, :, 0:8, :] = COURANT * ev[1, :, 0:8, :]
        hn[1, :, 0:8, :] = -COURANT * ev[0, :, 0:8, :]

    @pl.when(jnp.logical_not(low))
    def _():
        zl.wait_recv()
        hn[0:2, :, 0:8, :] = zl_r[...]

    sign = jnp.where(lane < 32, COURANT, -COURANT)
    mir = []
    for k in range(nchunk):
        z0 = zcs[k] * ZC
        yl[k].wait_recv()
        xl[k].wait_recv()
        ytile = jnp.where(gy == 0, sign * yu_s[k], yl_r[k])
        xl_r[k, 0] = jnp.where(gx == 0, COURANT * xu_s[k, 1], xl_r[k, 0])
        xl_r[k, 1] = jnp.where(gx == 0, -COURANT * xu_s[k, 0], xl_r[k, 1])
        design = k < nchunk - 1
        l0 = (z0 - jnp.where(low, ZC, 0)) if design else None
        for j in range(ZC):
            r = rows_at(z0 + j)
            hx, hy, hz = (plane(hn, c, r + 8) for c in range(3))
            hxz, hyz = (plane(hn, c, r) for c in range(2))

            def below_y(f, at):
                tile = pltpu.roll(ytile, PADL - 1 - at, 1)
                return pltpu.roll(jnp.concatenate([f, tile], 1), 1, 1)[:, :ny]

            def below_x(f, i):
                row = jnp.broadcast_to(xl_r[k, i, j : j + 1, :], (8, ny))
                return jnp.where(sub == 0, row, pltpu.roll(f, 1, 0))

            hzy, hxy = below_y(hz, j), below_y(hx, 32 + j)
            hyx, hzx = below_x(hy, 0), below_x(hz, 1)
            m = mv[pl.ds(r, 8), :]
            gain = inv[-1]
            for i in range(len(inv) - 2, -1, -1):
                gain = jnp.where(m == i, inv[i], gain)
            gain = COURANT * gain
            curl = (
                (hz - hzy) - (hy - hyz),
                (hx - hxz) - (hz - hzx),
                (hy - hyx) - (hx - hxy),
            )
            dot = None
            for c in range(3):
                e = plane(ev, c, r) + gain * curl[c]
                en[c, pl.ds(r, 8), :] = e
                if design:
                    term = fv[c, pl.ds(r, 8), :] * e
                    dot = term if dot is None else dot + term
            if design:
                lr = rows_at(l0 + j)
                put(gt, gsv[pl.ds(lr, 8), :] + mask * dot, lr)
        if design:
            for x in range(8):
                gsend[k, x] = strided(gt, rows_at(l0) + x)
            for s in range(2):
                cols = slice(s * half, (s + 1) * half)
                c = rcopy(
                    gsend.at[k, :, :, cols], gmir.at[k, :, :, cols],
                    m_ss.at[k, s], m_rs.at[k, s], mirror,
                )
                c.start()
                mir.append(c)
    sends += mir
    store(en, eo_hbm)
    for t in range(tiles):
        store(gt.at[t], gto_hbm.at[:, lanes(t)])

    halo = RADIUS - 1
    nk = nchunk - 1
    wp, wm, el, er = [], [], [], []
    for k in range(nk):
        for s in range(2):
            cols = slice(s * half, (s + 1) * half)
            mir[2 * k + s].wait_recv()
            for x in range(8):
                wide[k, halo + x, :, cols] = gsend[k, x, :, cols] + gmir[k, 7 - x, :, cols]
            c = rcopy(
                wide.at[k, 8 : 8 + halo, :, cols], wide.at[k, 0:halo, :, cols],
                wp_ss.at[k, s], wp_rs.at[k, s], dev(1, 0),
            )
            c.start()
            wp.append(c)
            c = rcopy(
                wide.at[k, halo : 2 * halo, :, cols],
                wide.at[k, halo + 8 : 2 * halo + 8, :, cols],
                wm_ss.at[k, s], wm_rs.at[k, s], dev(-1, 0),
            )
            c.start()
            wm.append(c)
        left, right = zero_tile, zero_tile
        for x in range(8):
            here = (lane // 8) == x
            t = wide[k, halo + x, :, 0:PADL]
            left = jnp.where(here, pltpu.roll(t, 8 * x, 1) if x else t, left)
            t = wide[k, halo + x, :, ny - PADL : ny]
            right = jnp.where(here, pltpu.roll(t, 8 * x + 8, 1), right)
        er_s[k] = right
        el_s[k] = left
        for d in (0, 1, -1):
            c = rcopy(
                er_s.at[k], el_r.at[k, 1 - d], el_ss.at[k, 1 - d], el_rs.at[k, 1 - d], dev(d, 1)
            )
            c.start()
            el.append(c)
            c = rcopy(
                el_s.at[k], er_r.at[k, 1 - d], er_ss.at[k, 1 - d], er_rs.at[k, 1 - d], dev(d, -1)
            )
            c.start()
            er.append(c)
    sends += wp + wm + el + er

    table = cone_table()
    for k in range(nk):
        for c in el[3 * k : 3 * k + 3] + er[3 * k : 3 * k + 3]:
            c.wait_recv()
        for slot in range(3):
            gone = (gx == 0) if slot == 0 else (gx == ngx - 1)
            no_left, no_right = gy == 0, gy == ngy - 1
            if slot != 1:
                no_left, no_right = no_left | gone, no_right | gone
            tl = jnp.where(no_left, 0.0, el_r[k, slot])
            tr = jnp.where(no_right, 0.0, er_r[k, slot])
            for x in range(8):
                w = halo + x + 8 * (slot - 1)
                if 0 <= w < 8 + 2 * halo:
                    a = pltpu.roll(tl, (PADL - 8 - 8 * x) % PADL, 1)
                    b = pltpu.roll(tr, (PADL - 8 * x) % PADL, 1) if x else tr
                    wide[k, w, :, ny:] = jnp.where(lane < 64, b, a)
        for c in wp[2 * k : 2 * k + 2] + wm[2 * k : 2 * k + 2]:
            c.wait_recv()

        @pl.when(gx == 0)
        def _():
            wide[k, 0:halo, :, :ny] = jnp.zeros((halo, 8, ny), F32)

        @pl.when(gx == ngx - 1)
        def _():
            wide[k, halo + 8 :, :, :ny] = jnp.zeros((halo, 8, ny), F32)

        l0 = zcs[k] * ZC - jnp.where(low, ZC, 0)

        def row(x, carry):
            pair = [wide[k, x + halo]]
            for a in range(1, halo + 1):
                pair.append(wide[k, x + halo + a] + wide[k, x + halo - a])
            total = None
            for b in range(halo + 1):
                acc = None
                for a in range(halo + 1):
                    weight = float(table[RADIUS + a, RADIUS + b])
                    if weight > 0.0:
                        term = weight * pair[a]
                        acc = term if acc is None else acc + term
                if b == 0:
                    total = acc[:, :ny]
                else:
                    total = total + (
                        pltpu.roll(acc, b, 1)[:, :ny] + pltpu.roll(acc, ny + PADL - b, 1)[:, :ny]
                    )
            for t in range(tiles):
                gf[t, pl.ds(rows_at(l0) + x, ZC, stride=8), :] = total[:, lanes(t)]
            return carry

        lax.fori_loop(0, 8, row, 0)
        lr = rows_at(l0)
        for t in range(tiles):
            store(gf.at[t, pl.ds(lr, 8 * ZC), :], gfo_hbm.at[pl.ds(lr, 8 * ZC), lanes(t)])

    pl.when(low)(zl.wait_send)
    pl.when(jnp.logical_not(low))(zu.wait_send)
    for c in sends:
        c.wait_send()
    for c in outs:
        c.wait()


def on_device(sizes, e, h, f, material, permittivity, design_mask, grad_sum):
    nz, nx, ny = material.shape
    lay = grad_sum.shape[0]
    rows, lrows = nz * nx, lay * nx
    nchunk, nk = nz // ZC, lay // ZC
    halo, nt = RADIUS - 1, ny // PADL
    hbm = pl.BlockSpec(memory_space=pl.ANY)
    dma = pltpu.SemaphoreType.DMA
    v = lambda *shape: pltpu.VMEM(shape, F32)
    outs = pl.pallas_call(
        functools.partial(kernel, sizes),
        out_shape=(
            jax.ShapeDtypeStruct((3, rows, ny), F32),
            jax.ShapeDtypeStruct((3, rows, ny), F32),
            jax.ShapeDtypeStruct((lrows, ny), F32),
            jax.ShapeDtypeStruct((lrows, ny), F32),
        ),
        in_specs=[
            hbm, hbm, hbm, hbm,
            pl.BlockSpec(memory_space=pltpu.SMEM),
            pl.BlockSpec(memory_space=pltpu.VMEM),
            hbm,
        ],
        out_specs=(hbm, hbm, hbm, hbm),
        scratch_shapes=[
            v(3, nt, rows + 8, PADL),
            v(3, rows, ny),
            v(3, rows, ny),
            pltpu.VMEM((rows, ny), jnp.int32),
            v(lrows, ny),
            v(3, nt, rows + 8, PADL),
            v(3, rows, ny),
            v(nt, lrows, PADL),
            v(nt, lrows, PADL),
            v(nchunk, 2, ZC, ny), v(nchunk, 2, ZC, ny),
            v(nchunk, 2, ZC, ny), v(nchunk, 2, ZC, ny),
            v(nchunk, 8, PADL), v(nchunk, 8, PADL),
            v(nchunk, 8, PADL), v(nchunk, 8, PADL),
            v(2, nt, 8, PADL), v(2, nt, 8, PADL),
            v(nk, 8, ZC, ny), v(nk, 8, ZC, ny),
            v(nk, 8 + 2 * halo, ZC, ny + PADL),
            v(nk, 8, PADL), v(nk, 8, PADL),
            v(nk, 3, 8, PADL), v(nk, 3, 8, PADL),
            dma((nt + 4,)), dma((2 * nt + 1 + nk * nt,)),
            dma((nchunk,)), dma((nchunk,)), dma((nchunk,)), dma((nchunk,)),
            dma((nchunk,)), dma((nchunk,)), dma((nchunk,)), dma((nchunk,)),
            dma((2,)), dma((2,)),
            dma((nk, 2)), dma((nk, 2)), dma((nk, 2)), dma((nk, 2)), dma((nk, 2)), dma((nk, 2)),
            dma((nk, 3)), dma((nk, 3)), dma((nk, 3)), dma((nk, 3)),
        ],
        compiler_params=pltpu.CompilerParams(
            collective_id=0, has_side_effects=True, vmem_limit_bytes=48 * 1024 * 1024
        ),
    )(
        e.reshape(3, rows, ny), h.reshape(3, rows, ny), f.reshape(3, rows, ny),
        material.reshape(rows, ny), permittivity, design_mask, grad_sum.reshape(lrows, ny),
    )
    return (
        outs[0].reshape(3, nz, nx, ny),
        outs[1].reshape(3, nz, nx, ny),
        outs[2].reshape(lay, nx, ny),
        outs[3].reshape(lay, nx, ny),
    )


def solution(mesh):
    field = P(None, "gz", "gx", "gy")
    cells = P("gz", "gx", "gy")
    return jax.shard_map(
        functools.partial(on_device, (mesh.shape["gx"], mesh.shape["gy"])),
        mesh=mesh,
        in_specs=(field, field, field, cells, P(), P("gx", "gy"), cells),
        out_specs=(field, field, cells, cells),
        check_vma=False,
    )
```

```python
import functools

import jax
import jax.numpy as jnp
import numpy as np
from jax import lax
from jax.experimental import pallas as pl
from jax.experimental.pallas import tpu as pltpu
from jax.sharding import PartitionSpec as P

RADIUS = 6
BLOCK = 8
COURANT = 0.5
MESH = pl.DeviceIdType.MESH
F32 = jnp.float32
ZC = 8
PADL = 128


def cone_table():
    span = np.arange(2 * RADIUS + 1, dtype=np.float32) - np.float32(RADIUS)
    dist = np.sqrt(span[:, None] ** 2 + span[None, :] ** 2).astype(np.float32)
    cone = np.maximum(np.float32(RADIUS) - dist, np.float32(0.0))
    return (cone / cone.sum(dtype=np.float32)).astype(np.float32)


def kernel(
    sizes,
    e_hbm, h_hbm, f_hbm, m_hbm, perm_ref, mask_ref, gs_hbm,
    en, hn, gt, gf, last,
    ev, hv, fv, mv, gsv,
    xu_s, xu_r, xl_s, xl_r, yu_s, yu_r, yl_s, yl_r, zu_r, zl_r,
    gsend, gmir, wide, el_s, er_s, el_r, er_r, q_s, q_m, sq, sq_p, sq_n,
    in_sem,
    xu_ss, xu_rs, xl_ss, xl_rs, yu_ss, yu_rs, yl_ss, yl_rs, z_ss, z_rs,
    m_ss, m_rs, wp_ss, wp_rs, wm_ss, wm_rs, el_ss, el_rs, er_ss, er_rs,
    q_ss, q_rs, sp_ss, sp_rs, sn_ss, sn_rs,
):
    ngx, ngy = sizes
    gx, gy, gz = lax.axis_index("gx"), lax.axis_index("gy"), lax.axis_index("gz")
    ny = hv.shape[-1]
    nchunk = m_hbm.shape[0] // (8 * ZC)
    rows = nchunk * ZC * 8
    half = ny // 2

    def dev(dx=0, dy=0):
        return {
            "gx": lax.rem(gx + (dx + ngx), ngx),
            "gy": lax.rem(gy + (dy + ngy), ngy),
            "gz": gz,
        }

    mirror = {"gx": ngx - 1 - gx, "gy": gy, "gz": gz}
    zother = {"gx": gx, "gy": gy, "gz": 1 - gz}

    def load(i, src, dst):
        c = pltpu.make_async_copy(src, dst, in_sem.at[i])
        c.start()
        return c

    tiles = ny // PADL

    def lanes(t):
        return slice(t * PADL, (t + 1) * PADL)

    def plane(ref, *at):
        lead, r = at[:-1], at[-1]
        return jnp.concatenate(
            [ref[(*lead, t, pl.ds(r, 8), slice(None))] for t in range(tiles)], 1
        )

    def put(ref, value, *at):
        lead, r = at[:-1], at[-1]
        for t in range(tiles):
            ref[(*lead, t, pl.ds(r, 8), slice(None))] = value[:, lanes(t)]

    def strided(ref, *at):
        lead, r = at[:-1], at[-1]
        return jnp.concatenate(
            [ref[(*lead, t, pl.ds(r, 8, stride=8), slice(None))] for t in range(tiles)], 1
        )

    c_e = [load(t, e_hbm.at[:, :, lanes(t)], ev.at[:, t, 0:rows, :]) for t in range(tiles)]
    c_h = load(tiles, h_hbm, hv)
    c_m = load(tiles + 1, m_hbm, mv)
    c_f = load(tiles + 2, f_hbm, fv)
    c_g = load(tiles + 3, gs_hbm, gsv)

    barrier = pltpu.get_barrier_semaphore()
    peers = [dev(-1, 0), dev(1, 0), dev(0, -1), dev(0, 1), mirror, zother]
    for peer in peers:
        pl.semaphore_signal(barrier, inc=1, device_id=peer, device_id_type=MESH)

    sub = lax.broadcasted_iota(jnp.int32, (8, ny), 0)
    lane = lax.broadcasted_iota(jnp.int32, (8, PADL), 1)
    zero_tile = jnp.zeros((8, PADL), F32)

    low = gz == 0
    zcs = [jnp.where(low, nchunk - 1 - k, k) for k in range(nchunk)]

    def rows_at(z):
        return pl.multiple_of(z * 8, 8)

    nblk = mask_ref.shape[1]
    spread = (
        lax.broadcasted_iota(jnp.int32, (nblk, ny), 1) // BLOCK
        == lax.broadcasted_iota(jnp.int32, (nblk, ny), 0)
    ).astype(F32)
    mask = jnp.dot(
        jnp.broadcast_to(mask_ref[...].astype(F32), (8, nblk)), spread, preferred_element_type=F32
    )
    inv = [1.0 / jnp.full((8, ny), perm_ref[i], F32) for i in range(perm_ref.shape[0])]

    def rcopy(src, dst, ss, rs, peer):
        return pltpu.make_async_remote_copy(
            src_ref=src, dst_ref=dst, send_sem=ss, recv_sem=rs, device_id=peer, device_id_type=MESH
        )

    sends = []
    for c in c_e:
        c.wait()
    xu, yu = [], []
    for k in range(nchunk):
        z0 = zcs[k] * ZC
        for i, c in enumerate((1, 2)):
            xu_s[k, i] = strided(ev, c, rows_at(z0))
        acc = zero_tile
        for j in range(ZC):
            r = rows_at(z0 + j)
            for i, c in enumerate((0, 2)):
                tile = ev[c, 0, pl.ds(r, 8), :]
                at = 32 * i + j
                acc = jnp.where(lane == at, pltpu.roll(tile, at, 1) if at else tile, acc)
        yu_s[k] = acc
    pl.semaphore_wait(barrier, len(peers))
    zu = rcopy(ev.at[0:2, :, 0:8, :], zu_r, z_ss.at[0], z_rs.at[0], zother)
    pl.when(jnp.logical_not(low))(zu.start)
    for k in range(nchunk):
        c = rcopy(yu_s.at[k], yu_r.at[k], yu_ss.at[k], yu_rs.at[k], dev(0, -1))
        c.start()
        yu.append(c)
        c = rcopy(xu_s.at[k], xu_r.at[k], xu_ss.at[k], xu_rs.at[k], dev(-1, 0))
        c.start()
        xu.append(c)
    sends += yu + xu

    c_h.wait()

    @pl.when(low)
    def _():
        zu.wait_recv()
        ev[0:2, :, rows : rows + 8, :] = zu_r[...]

    @pl.when(jnp.logical_not(low))
    def _():
        ev[0:2, :, rows : rows + 8, :] = jnp.zeros((2, tiles, 8, PADL), F32)

    xl, yl = [], []
    zl = None
    for k in range(nchunk):
        z0 = zcs[k] * ZC
        yu[k].wait_recv()
        xu[k].wait_recv()
        ytile = jnp.where(gy == ngy - 1, 0.0, yu_r[k])
        xu_r[k] = jnp.where(gx == ngx - 1, 0.0, xu_r[k])
        acc = zero_tile
        for j in range(ZC):
            r = rows_at(z0 + j)
            ex, ey, ez = (plane(ev, c, r) for c in range(3))
            exz, eyz = (plane(ev, c, r + 8) for c in range(2))
            hx, hy, hz = (hv[c, pl.ds(r, 8), :] for c in range(3))

            def above_y(f, at):
                tile = pltpu.roll(ytile, (PADL - at) % PADL, 1) if at else ytile
                return pltpu.roll(jnp.concatenate([f, tile], 1), ny + PADL - 1, 1)[:, :ny]

            def above_x(f, i):
                row = jnp.broadcast_to(xu_r[k, i, j : j + 1, :], (8, ny))
                return jnp.where(sub == 7, row, pltpu.roll(f, 7, 0))

            exy, ezy = above_y(ex, j), above_y(ez, 32 + j)
            eyx, ezx = above_x(ey, 0), above_x(ez, 1)
            hxn = hx - COURANT * ((ezy - ez) - (eyz - ey))
            hyn = hy - COURANT * ((exz - ex) - (ezx - ez))
            hzn = hz - COURANT * ((eyx - ey) - (exy - ex))
            for c, h in enumerate((hxn, hyn, hzn)):
                put(hn, h, c, r + 8)
            for i, h in enumerate((hzn, hxn)):
                at = 32 * i + j
                rolled = pltpu.roll(h[:, ny - PADL :], at + 1, 1)
                acc = jnp.where(lane == at, rolled, acc)
        yl_s[k] = acc
        for i, c in enumerate((1, 2)):
            xl_s[k, i] = strided(hn, c, rows_at(z0 + 1) + 7)
        if k == 0:
            zl = rcopy(hn.at[0:2, :, rows : rows + 8, :], zl_r, z_ss.at[1], z_rs.at[1], zother)
        c = rcopy(yl_s.at[k], yl_r.at[k], yl_ss.at[k], yl_rs.at[k], dev(0, 1))
        c.start()
        yl.append(c)
        c = rcopy(xl_s.at[k], xl_r.at[k], xl_ss.at[k], xl_rs.at[k], dev(1, 0))
        c.start()
        xl.append(c)
        if k == 0:
            pl.when(low)(zl.start)

    sends += yl + xl

    c_m.wait()
    c_f.wait()
    c_g.wait()

    @pl.when(low)
    def _():
        hn[0, :, 0:8, :] = COURANT * ev[1, :, 0:8, :]
        hn[1, :, 0:8, :] = -COURANT * ev[0, :, 0:8, :]

    @pl.when(jnp.logical_not(low))
    def _():
        zl.wait_recv()
        hn[0:2, :, 0:8, :] = zl_r[...]

    sign = jnp.where(lane < 32, COURANT, -COURANT)
    mir, el, er, qm = [], [], [], []
    for k in range(nchunk):
        z0 = zcs[k] * ZC
        yl[k].wait_recv()
        xl[k].wait_recv()
        ytile = jnp.where(gy == 0, sign * yu_s[k], yl_r[k])
        xl_r[k, 0] = jnp.where(gx == 0, COURANT * xu_s[k, 1], xl_r[k, 0])
        xl_r[k, 1] = jnp.where(gx == 0, -COURANT * xu_s[k, 0], xl_r[k, 1])
        design = k < nchunk - 1
        l0 = (z0 - jnp.where(low, ZC, 0)) if design else None
        for j in range(ZC):
            r = rows_at(z0 + j)
            hx, hy, hz = (plane(hn, c, r + 8) for c in range(3))
            hxz, hyz = (plane(hn, c, r) for c in range(2))

            def below_y(f, at):
                tile = pltpu.roll(ytile, PADL - 1 - at, 1)
                return pltpu.roll(jnp.concatenate([f, tile], 1), 1, 1)[:, :ny]

            def below_x(f, i):
                row = jnp.broadcast_to(xl_r[k, i, j : j + 1, :], (8, ny))
                return jnp.where(sub == 0, row, pltpu.roll(f, 1, 0))

            hzy, hxy = below_y(hz, j), below_y(hx, 32 + j)
            hyx, hzx = below_x(hy, 0), below_x(hz, 1)
            m = mv[pl.ds(r, 8), :]
            gain = inv[-1]
            for i in range(len(inv) - 2, -1, -1):
                gain = jnp.where(m == i, inv[i], gain)
            gain = COURANT * gain
            curl = (
                (hz - hzy) - (hy - hyz),
                (hx - hxz) - (hz - hzx),
                (hy - hyx) - (hx - hxy),
            )
            dot = None
            for c in range(3):
                e = plane(ev, c, r) + gain * curl[c]
                en[c, pl.ds(r, 8), :] = e
                if design:
                    term = fv[c, pl.ds(r, 8), :] * e
                    dot = term if dot is None else dot + term
            if design:
                lr = rows_at(l0 + j)
                put(gt, gsv[pl.ds(lr, 8), :] + mask * dot, lr)
        if design:
            left, right = zero_tile, zero_tile
            for x in range(8):
                g = strided(gt, rows_at(l0) + x)
                gsend[k, x] = g
                here = (lane // 8) == x
                t = g[:, :PADL]
                left = jnp.where(here, pltpu.roll(t, 8 * x, 1) if x else t, left)
                right = jnp.where(here, pltpu.roll(g[:, ny - PADL :], 8 * x + 8, 1), right)
            er_s[k] = right
            el_s[k] = left
            c = rcopy(er_s.at[k], el_r.at[k], el_ss.at[k], el_rs.at[k], dev(0, 1))
            c.start()
            el.append(c)
            c = rcopy(el_s.at[k], er_r.at[k], er_ss.at[k], er_rs.at[k], dev(0, -1))
            c.start()
            er.append(c)
            for s in range(2):
                cols = slice(s * half, (s + 1) * half)
                c = rcopy(
                    gsend.at[k, :, :, cols], gmir.at[k, :, :, cols],
                    m_ss.at[k, s], m_rs.at[k, s], mirror,
                )
                c.start()
                mir.append(c)
    for k in range(nchunk - 1):
        el[k].wait_recv()
        er[k].wait_recv()
        beyond_left = jnp.where(gy == 0, 0.0, el_r[k])
        beyond_right = jnp.where(gy == ngy - 1, 0.0, er_r[k])
        q_s[k] = jnp.where(lane < 64, beyond_left, pltpu.roll(beyond_right, 64, 1))
        c = rcopy(q_s.at[k], q_m.at[k], q_ss.at[k], q_rs.at[k], mirror)
        c.start()
        qm.append(c)
    sends += mir + el + er + qm

    halo = RADIUS - 1
    nk = nchunk - 1
    wp, wm, sp, sn = [], [], [], []
    for k in range(nk):
        qm[k].wait_recv()
        flipped = zero_tile
        for x in range(8):
            here = ((lane // 8) % 8) == x
            flipped = jnp.where(here, pltpu.roll(q_m[k], (8 * (2 * x - 7)) % PADL, 1), flipped)
        sq[k] = q_s[k] + flipped
        c = rcopy(sq.at[k], sq_p.at[k], sp_ss.at[k], sp_rs.at[k], dev(1, 0))
        c.start()
        sp.append(c)
        c = rcopy(sq.at[k], sq_n.at[k], sn_ss.at[k], sn_rs.at[k], dev(-1, 0))
        c.start()
        sn.append(c)
        for s in range(2):
            cols = slice(s * half, (s + 1) * half)
            mir[2 * k + s].wait_recv()
            for x in range(8):
                wide[k, halo + x, :, cols] = gsend[k, x, :, cols] + gmir[k, 7 - x, :, cols]
            c = rcopy(
                wide.at[k, 8 : 8 + halo, :, cols], wide.at[k, 0:halo, :, cols],
                wp_ss.at[k, s], wp_rs.at[k, s], dev(1, 0),
            )
            c.start()
            wp.append(c)
            c = rcopy(
                wide.at[k, halo : 2 * halo, :, cols],
                wide.at[k, halo + 8 : 2 * halo + 8, :, cols],
                wm_ss.at[k, s], wm_rs.at[k, s], dev(-1, 0),
            )
            c.start()
            wm.append(c)
    sends += wp + wm + sp + sn

    for k in range(nk):
        sp[k].wait_recv()
        sn[k].wait_recv()
        packs = (
            jnp.where(gx == 0, 0.0, sq_p[k]),
            sq[k],
            jnp.where(gx == ngx - 1, 0.0, sq_n[k]),
        )
        for w in range(8 + 2 * halo):
            slot, x = (w - halo + 8) // 8, (w - halo) % 8
            a = pltpu.roll(packs[slot], (PADL - 8 - 8 * x) % PADL, 1)
            b = pltpu.roll(packs[slot], 64 - 8 * x, 1)
            wide[k, w, :, ny:] = jnp.where(lane < 64, b, a)
        for c in wp[2 * k : 2 * k + 2] + wm[2 * k : 2 * k + 2]:
            c.wait_recv()

        @pl.when(gx == 0)
        def _():
            wide[k, 0:halo, :, :ny] = jnp.zeros((halo, 8, ny), F32)

        @pl.when(gx == ngx - 1)
        def _():
            wide[k, halo + 8 :, :, :ny] = jnp.zeros((halo, 8, ny), F32)

        if k < nk - 1:
            smooth(wide.at[k], gf)
        else:
            last[...] = wide[k]

    pl.when(low)(zl.wait_send)
    pl.when(jnp.logical_not(low))(zu.wait_send)
    for c in sends:
        c.wait_send()


def smooth(rows_ref, out_ref):
    table = cone_table()
    halo, tiles = RADIUS - 1, out_ref.shape[0]
    ny = tiles * PADL

    def row(x, carry):
        pair = [rows_ref[x + halo]]
        for a in range(1, halo + 1):
            pair.append(rows_ref[x + halo + a] + rows_ref[x + halo - a])
        total = None
        for b in range(halo + 1):
            acc = None
            for a in range(halo + 1):
                weight = float(table[RADIUS + a, RADIUS + b])
                if weight > 0.0:
                    term = weight * pair[a]
                    acc = term if acc is None else acc + term
            if b == 0:
                total = acc[:, :ny]
            else:
                total = total + (
                    pltpu.roll(acc, b, 1)[:, :ny] + pltpu.roll(acc, ny + PADL - b, 1)[:, :ny]
                )
        for t in range(tiles):
            out_ref[t, pl.ds(x, ZC, stride=8), :] = total[:, t * PADL : (t + 1) * PADL]
        return carry

    lax.fori_loop(0, 8, row, 0)


def finish(en, hn, gt, gf, last, eo, ho, gto, gfo, gl, sem):
    tiles, rows = gt.shape[0], en.shape[1]
    low = lax.axis_index("gz") == 0
    outs = []

    def store(src, dst):
        c = pltpu.make_async_copy(src, dst, sem.at[len(outs)])
        c.start()
        outs.append(c)

    n = 8 * ZC
    first = pl.multiple_of(jnp.where(low, n, 0), n)
    store(en, eo)
    for t in range(tiles):
        cols = slice(t * PADL, (t + 1) * PADL)
        store(hn.at[:, t, 8 : rows + 8, :], ho.at[:, :, cols])
        store(gt.at[t], gto.at[:, cols])
        store(gf.at[t], gfo.at[pl.ds(first, n), cols])
    smooth(last, gl)
    for t in range(tiles):
        cols = slice(t * PADL, (t + 1) * PADL)
        store(gl.at[t], gfo.at[pl.ds(n - first, n), cols])
    for c in outs:
        c.wait()


def on_device(sizes, e, h, f, material, permittivity, design_mask, grad_sum):
    nz, nx, ny = material.shape
    lay = grad_sum.shape[0]
    rows, lrows = nz * nx, lay * nx
    nchunk, nk = nz // ZC, lay // ZC
    halo, nt = RADIUS - 1, ny // PADL
    hbm = pl.BlockSpec(memory_space=pltpu.HBM)
    vmem = pl.BlockSpec(memory_space=pltpu.VMEM)
    dma = pltpu.SemaphoreType.DMA
    v = lambda *shape: pltpu.VMEM(shape, F32)
    mid = pl.pallas_call(
        functools.partial(kernel, sizes),
        out_shape=(
            v(3, rows, ny),
            v(3, nt, rows + 8, PADL),
            v(nt, lrows, PADL),
            v(nt, 8 * ZC, PADL),
            v(8 + 2 * halo, ZC, ny + PADL),
        ),
        in_specs=[
            hbm, hbm, hbm, hbm,
            pl.BlockSpec(memory_space=pltpu.SMEM),
            pl.BlockSpec(memory_space=pltpu.VMEM),
            hbm,
        ],
        out_specs=(vmem,) * 5,
        scratch_shapes=[
            v(3, nt, rows + 8, PADL),
            v(3, rows, ny),
            v(3, rows, ny),
            pltpu.VMEM((rows, ny), jnp.int32),
            v(lrows, ny),
            v(nchunk, 2, ZC, ny), v(nchunk, 2, ZC, ny),
            v(nchunk, 2, ZC, ny), v(nchunk, 2, ZC, ny),
            v(nchunk, 8, PADL), v(nchunk, 8, PADL),
            v(nchunk, 8, PADL), v(nchunk, 8, PADL),
            v(2, nt, 8, PADL), v(2, nt, 8, PADL),
            v(nk, 8, ZC, ny), v(nk, 8, ZC, ny),
            v(nk, 8 + 2 * halo, ZC, ny + PADL),
            v(nk, 8, PADL), v(nk, 8, PADL),
            v(nk, 8, PADL), v(nk, 8, PADL),
            v(nk, 8, PADL), v(nk, 8, PADL), v(nk, 8, PADL), v(nk, 8, PADL), v(nk, 8, PADL),
            dma((nt + 4,)),
            dma((nchunk,)), dma((nchunk,)), dma((nchunk,)), dma((nchunk,)),
            dma((nchunk,)), dma((nchunk,)), dma((nchunk,)), dma((nchunk,)),
            dma((2,)), dma((2,)),
            dma((nk, 2)), dma((nk, 2)), dma((nk, 2)), dma((nk, 2)), dma((nk, 2)), dma((nk, 2)),
            dma((nk,)), dma((nk,)), dma((nk,)), dma((nk,)),
            dma((nk,)), dma((nk,)), dma((nk,)), dma((nk,)), dma((nk,)), dma((nk,)),
        ],
        compiler_params=pltpu.CompilerParams(
            collective_id=0, has_side_effects=True, vmem_limit_bytes=63_500_000
        ),
    )(
        e.reshape(3, rows, ny), h.reshape(3, rows, ny), f.reshape(3, rows, ny),
        material.reshape(rows, ny), permittivity, design_mask, grad_sum.reshape(lrows, ny),
    )
    outs = pl.pallas_call(
        finish,
        out_shape=(
            jax.ShapeDtypeStruct((3, rows, ny), F32),
            jax.ShapeDtypeStruct((3, rows, ny), F32),
            jax.ShapeDtypeStruct((lrows, ny), F32),
            jax.ShapeDtypeStruct((lrows, ny), F32),
        ),
        in_specs=[vmem] * 5,
        out_specs=(hbm,) * 4,
        scratch_shapes=[v(nt, 8 * ZC, PADL), dma((1 + 4 * nt,))],
        compiler_params=pltpu.CompilerParams(vmem_limit_bytes=32 * 1024 * 1024),
    )(*mid)
    return (
        outs[0].reshape(3, nz, nx, ny),
        outs[1].reshape(3, nz, nx, ny),
        outs[2].reshape(lay, nx, ny),
        outs[3].reshape(lay, nx, ny),
    )


def solution(mesh):
    field = P(None, "gz", "gx", "gy")
    cells = P("gz", "gx", "gy")
    return jax.shard_map(
        functools.partial(on_device, (mesh.shape["gx"], mesh.shape["gy"])),
        mesh=mesh,
        in_specs=(field, field, field, cells, P(), P("gx", "gy"), cells),
        out_specs=(field, field, cells, cells),
        check_vma=False,
    )
```

```python
import functools

import jax
import jax.numpy as jnp
import numpy as np
from jax import lax
from jax.experimental import pallas as pl
from jax.experimental.pallas import tpu as pltpu
from jax.sharding import PartitionSpec as P

RADIUS = 6
BLOCK = 8
COURANT = 0.5
MESH = pl.DeviceIdType.MESH
F32 = jnp.float32
ZC = 8
PADL = 128


def cone_table():
    span = np.arange(2 * RADIUS + 1, dtype=np.float32) - np.float32(RADIUS)
    dist = np.sqrt(span[:, None] ** 2 + span[None, :] ** 2).astype(np.float32)
    cone = np.maximum(np.float32(RADIUS) - dist, np.float32(0.0))
    return (cone / cone.sum(dtype=np.float32)).astype(np.float32)


def kernel(
    sizes,
    e_hbm, h_hbm, f_hbm, m_hbm, perm_hbm, mask_hbm, gs_hbm,
    en, hn, gt, gf, last,
    ev, hv, fv, mv, gsv, perm_ref, mask_ref,
    xu_s, xu_r, xl_s, xl_r, yu_s, yu_r, yl_s, yl_r, zu_r, zl_r,
    gsend, gmir, wide, el_s, er_s, el_r, er_r, q_s, q_m, sq, sq_p, sq_n, turned,
    in_sem,
    xu_ss, xu_rs, xl_ss, xl_rs, yu_ss, yu_rs, yl_ss, yl_rs, z_ss, z_rs,
    m_ss, m_rs, wp_ss, wp_rs, wm_ss, wm_rs, el_ss, el_rs, er_ss, er_rs,
    q_ss, q_rs, sp_ss, sp_rs, sn_ss, sn_rs,
):
    ngx, ngy = sizes
    gx, gy, gz = lax.axis_index("gx"), lax.axis_index("gy"), lax.axis_index("gz")
    ny = hv.shape[-1]
    nchunk = m_hbm.shape[0] // (8 * ZC)
    rows = nchunk * ZC * 8
    half = ny // 2

    def dev(dx=0, dy=0):
        return {
            "gx": lax.rem(gx + (dx + ngx), ngx),
            "gy": lax.rem(gy + (dy + ngy), ngy),
            "gz": gz,
        }

    mirror = {"gx": ngx - 1 - gx, "gy": gy, "gz": gz}
    zother = {"gx": gx, "gy": gy, "gz": 1 - gz}

    even = lax.rem(gx, 2) == 0
    image_at = jnp.where(even, ngx, ngx - 2) - gx
    own_image = image_at == gx
    has_image = (gx != 0) & (gx != ngx - 1) & jnp.logical_not(own_image)
    image = {"gx": lax.rem(image_at + ngx, ngx), "gy": gy, "gz": gz}

    barrier = pltpu.get_barrier_semaphore()
    peers = [dev(-1, 0), dev(1, 0), dev(0, -1), dev(0, 1), mirror, zother]
    for peer in peers:
        pl.semaphore_signal(barrier, inc=1, device_id=peer, device_id_type=MESH)

    @pl.when(has_image)
    def _():
        pl.semaphore_signal(barrier, inc=1, device_id=image, device_id_type=MESH)


    def load(i, src, dst):
        c = pltpu.make_async_copy(src, dst, in_sem.at[i])
        c.start()
        return c

    tiles = ny // PADL

    def lanes(t):
        return slice(t * PADL, (t + 1) * PADL)

    def plane(ref, *at):
        lead, r = at[:-1], at[-1]
        return jnp.concatenate(
            [ref[(*lead, t, pl.ds(r, 8), slice(None))] for t in range(tiles)], 1
        )

    def put(ref, value, *at):
        lead, r = at[:-1], at[-1]
        for t in range(tiles):
            ref[(*lead, t, pl.ds(r, 8), slice(None))] = value[:, lanes(t)]

    def strided(ref, *at):
        lead, r = at[:-1], at[-1]
        return jnp.concatenate(
            [ref[(*lead, t, pl.ds(r, 8, stride=8), slice(None))] for t in range(tiles)], 1
        )

    c_e = [load(t, e_hbm.at[:, :, lanes(t)], ev.at[:, t, 0:rows, :]) for t in range(tiles)]
    c_h = load(tiles, h_hbm, hv)
    c_m = load(tiles + 1, m_hbm, mv)
    c_f = load(tiles + 2, f_hbm, fv)
    c_p = load(tiles + 4, perm_hbm, perm_ref)
    c_k = load(tiles + 5, mask_hbm, mask_ref)
    c_g = load(tiles + 3, gs_hbm, gsv)

    sub = lax.broadcasted_iota(jnp.int32, (8, ny), 0)
    lane = lax.broadcasted_iota(jnp.int32, (8, PADL), 1)
    zero_tile = jnp.zeros((8, PADL), F32)

    low = gz == 0
    zcs = [jnp.where(low, nchunk - 1 - k, k) for k in range(nchunk)]

    def rows_at(z):
        return pl.multiple_of(z * 8, 8)

    def rcopy(src, dst, ss, rs, peer):
        return pltpu.make_async_remote_copy(
            src_ref=src, dst_ref=dst, send_sem=ss, recv_sem=rs, device_id=peer, device_id_type=MESH
        )

    sends = []
    for c in c_e:
        c.wait()
    xu = []
    for k in range(nchunk):
        z0 = zcs[k] * ZC
        for i, c in enumerate((1, 2)):
            xu_s[k, i] = strided(ev, c, rows_at(z0))
        acc = zero_tile
        for j in range(ZC):
            r = rows_at(z0 + j)
            for i, c in enumerate((0, 2)):
                tile = ev[c, 0, pl.ds(r, 8), :]
                at = 32 * i + j
                acc = jnp.where(lane == at, pltpu.roll(tile, at, 1) if at else tile, acc)
        yu_s[k] = acc
    pl.semaphore_wait(barrier, len(peers) + has_image.astype(jnp.int32))
    yu = rcopy(yu_s, yu_r, yu_ss.at[0], yu_rs.at[0], dev(0, -1))
    yu.start()
    zu = rcopy(ev.at[0:2, :, 0:8, :], zu_r, z_ss.at[0], z_rs.at[0], zother)
    pl.when(jnp.logical_not(low))(zu.start)
    for k in range(nchunk):
        c = rcopy(xu_s.at[k], xu_r.at[k], xu_ss.at[k], xu_rs.at[k], dev(-1, 0))
        c.start()
        xu.append(c)
    sends += [yu] + xu

    c_p.wait()
    c_k.wait()
    nblk = mask_ref.shape[1]
    spread = (
        lax.broadcasted_iota(jnp.int32, (nblk, ny), 1) // BLOCK
        == lax.broadcasted_iota(jnp.int32, (nblk, ny), 0)
    ).astype(F32)
    mask = jnp.dot(
        jnp.broadcast_to(mask_ref[...].astype(F32), (8, nblk)), spread, preferred_element_type=F32
    )
    inv = [1.0 / jnp.full((8, ny), perm_ref[i], F32) for i in range(perm_ref.shape[0])]

    c_h.wait()

    @pl.when(low)
    def _():
        zu.wait_recv()
        ev[0:2, :, rows : rows + 8, :] = zu_r[...]

    @pl.when(jnp.logical_not(low))
    def _():
        ev[0:2, :, rows : rows + 8, :] = jnp.zeros((2, tiles, 8, PADL), F32)

    xl, yl = [], []
    zl = None
    for k in range(nchunk):
        z0 = zcs[k] * ZC
        if k == 0:
            yu.wait_recv()
        xu[k].wait_recv()
        ytile = jnp.where(gy == ngy - 1, 0.0, yu_r[k])
        xu_r[k] = jnp.where(gx == ngx - 1, 0.0, xu_r[k])
        acc = zero_tile
        for j in range(ZC):
            r = rows_at(z0 + j)
            ex, ey, ez = (plane(ev, c, r) for c in range(3))
            exz, eyz = (plane(ev, c, r + 8) for c in range(2))
            hx, hy, hz = (hv[c, pl.ds(r, 8), :] for c in range(3))

            def above_y(f, at):
                tile = pltpu.roll(ytile, (PADL - at) % PADL, 1) if at else ytile
                return pltpu.roll(jnp.concatenate([f, tile], 1), ny + PADL - 1, 1)[:, :ny]

            def above_x(f, i):
                row = jnp.broadcast_to(xu_r[k, i, j : j + 1, :], (8, ny))
                return jnp.where(sub == 7, row, pltpu.roll(f, 7, 0))

            exy, ezy = above_y(ex, j), above_y(ez, 32 + j)
            eyx, ezx = above_x(ey, 0), above_x(ez, 1)
            hxn = hx - COURANT * ((ezy - ez) - (eyz - ey))
            hyn = hy - COURANT * ((exz - ex) - (ezx - ez))
            hzn = hz - COURANT * ((eyx - ey) - (exy - ex))
            for c, h in enumerate((hxn, hyn, hzn)):
                put(hn, h, c, r + 8)
            for i, h in enumerate((hzn, hxn)):
                at = 32 * i + j
                rolled = pltpu.roll(h[:, ny - PADL :], at + 1, 1)
                acc = jnp.where(lane == at, rolled, acc)
        yl_s[k] = acc
        for i, c in enumerate((1, 2)):
            xl_s[k, i] = strided(hn, c, rows_at(z0 + 1) + 7)
        if k == 0:
            zl = rcopy(hn.at[0:2, :, rows : rows + 8, :], zl_r, z_ss.at[1], z_rs.at[1], zother)
        c = rcopy(yl_s.at[k], yl_r.at[k], yl_ss.at[k], yl_rs.at[k], dev(0, 1))
        c.start()
        yl.append(c)
        c = rcopy(xl_s.at[k], xl_r.at[k], xl_ss.at[k], xl_rs.at[k], dev(1, 0))
        c.start()
        xl.append(c)
        if k == 0:
            pl.when(low)(zl.start)

    sends += yl + xl

    c_m.wait()
    c_f.wait()
    c_g.wait()

    @pl.when(low)
    def _():
        hn[0, :, 0:8, :] = COURANT * ev[1, :, 0:8, :]
        hn[1, :, 0:8, :] = -COURANT * ev[0, :, 0:8, :]

    @pl.when(jnp.logical_not(low))
    def _():
        zl.wait_recv()
        hn[0:2, :, 0:8, :] = zl_r[...]

    sign = jnp.where(lane < 32, COURANT, -COURANT)
    mir, el, er, qm = [], [], [], []
    for k in range(nchunk):
        z0 = zcs[k] * ZC
        yl[k].wait_recv()
        xl[k].wait_recv()
        ytile = jnp.where(gy == 0, sign * yu_s[k], yl_r[k])
        xl_r[k, 0] = jnp.where(gx == 0, COURANT * xu_s[k, 1], xl_r[k, 0])
        xl_r[k, 1] = jnp.where(gx == 0, -COURANT * xu_s[k, 0], xl_r[k, 1])
        design = k < nchunk - 1
        l0 = (z0 - jnp.where(low, ZC, 0)) if design else None
        for j in range(ZC):
            r = rows_at(z0 + j)
            hx, hy, hz = (plane(hn, c, r + 8) for c in range(3))
            hxz, hyz = (plane(hn, c, r) for c in range(2))

            def below_y(f, at):
                tile = pltpu.roll(ytile, PADL - 1 - at, 1)
                return pltpu.roll(jnp.concatenate([f, tile], 1), 1, 1)[:, :ny]

            def below_x(f, i):
                row = jnp.broadcast_to(xl_r[k, i, j : j + 1, :], (8, ny))
                return jnp.where(sub == 0, row, pltpu.roll(f, 1, 0))

            hzy, hxy = below_y(hz, j), below_y(hx, 32 + j)
            hyx, hzx = below_x(hy, 0), below_x(hz, 1)
            m = mv[pl.ds(r, 8), :]
            gain = inv[-1]
            for i in range(len(inv) - 2, -1, -1):
                gain = jnp.where(m == i, inv[i], gain)
            gain = COURANT * gain
            curl = (
                (hz - hzy) - (hy - hyz),
                (hx - hxz) - (hz - hzx),
                (hy - hyx) - (hx - hxy),
            )
            dot = None
            for c in range(3):
                e = plane(ev, c, r) + gain * curl[c]
                en[c, pl.ds(r, 8), :] = e
                if design:
                    term = fv[c, pl.ds(r, 8), :] * e
                    dot = term if dot is None else dot + term
            if design:
                lr = rows_at(l0 + j)
                put(gt, gsv[pl.ds(lr, 8), :] + mask * dot, lr)
        if design:
            left, right = zero_tile, zero_tile
            for x in range(8):
                g = strided(gt, rows_at(l0) + x)
                gsend[k, x] = g
                here = (lane // 8) == x
                t = g[:, :PADL]
                left = jnp.where(here, pltpu.roll(t, 8 * x, 1) if x else t, left)
                right = jnp.where(here, pltpu.roll(g[:, ny - PADL :], 8 * x + 8, 1), right)
            er_s[k] = right
            el_s[k] = left
            c = rcopy(er_s.at[k], el_r.at[k], el_ss.at[k], el_rs.at[k], dev(0, 1))
            c.start()
            el.append(c)
            c = rcopy(el_s.at[k], er_r.at[k], er_ss.at[k], er_rs.at[k], dev(0, -1))
            c.start()
            er.append(c)
            for s in range(2):
                cols = slice(s * half, (s + 1) * half)
                c = rcopy(
                    gsend.at[k, :, :, cols], gmir.at[k, :, :, cols],
                    m_ss.at[k, s], m_rs.at[k, s], mirror,
                )
                c.start()
                mir.append(c)
    for k in range(nchunk - 1):
        el[k].wait_recv()
        er[k].wait_recv()
        beyond_left = jnp.where(gy == 0, 0.0, el_r[k])
        beyond_right = jnp.where(gy == ngy - 1, 0.0, er_r[k])
        q_s[k] = jnp.where(lane < 64, beyond_left, pltpu.roll(beyond_right, 64, 1))
        c = rcopy(q_s.at[k], q_m.at[k], q_ss.at[k], q_rs.at[k], mirror)
        c.start()
        qm.append(c)
    sends += mir + el + er + qm

    halo = RADIUS - 1
    nk = nchunk - 1
    wp, wm, sp, sn = [], [], [], []
    for k in range(nk):
        qm[k].wait_recv()
        flipped = zero_tile
        for x in range(8):
            here = ((lane // 8) % 8) == x
            flipped = jnp.where(here, pltpu.roll(q_m[k], (8 * (2 * x - 7)) % PADL, 1), flipped)
        sq[k] = q_s[k] + flipped
        c = rcopy(sq.at[k], sq_p.at[k], sp_ss.at[k], sp_rs.at[k], dev(1, 0))
        c.start()
        sp.append(c)
        c = rcopy(sq.at[k], sq_n.at[k], sn_ss.at[k], sn_rs.at[k], dev(-1, 0))
        c.start()
        sn.append(c)
        for s in range(2):
            cols = slice(s * half, (s + 1) * half)
            mir[2 * k + s].wait_recv()
            for x in range(8):
                wide[k, halo + x, :, cols] = gsend[k, x, :, cols] + gmir[k, 7 - x, :, cols]
            if k < nk - 1:
                c = rcopy(
                    wide.at[k, 8 : 8 + halo, :, cols], wide.at[k, 0:halo, :, cols],
                    wp_ss.at[k, s], wp_rs.at[k, s], dev(1, 0),
                )
                c.start()
                wp.append(c)
                c = rcopy(
                    wide.at[k, halo : 2 * halo, :, cols],
                    wide.at[k, halo + 8 : 2 * halo + 8, :, cols],
                    wm_ss.at[k, s], wm_rs.at[k, s], dev(-1, 0),
                )
                c.start()
                wm.append(c)
            else:
                for i in range(halo):
                    turned[i, :, cols] = wide[k, halo + jnp.where(even, halo - 1, 7) - i, :, cols]
                land = pl.ds(jnp.where(even, 0, halo + 8), halo)
                c = rcopy(
                    turned.at[:, :, cols], wide.at[k, land, :, cols],
                    wm_ss.at[k, s], wm_rs.at[k, s], image,
                )
                pl.when(has_image)(c.start)
                wm.append(c)

                @pl.when(own_image)
                def _():
                    wide[k, land, :, cols] = turned[:, :, cols]

                c = rcopy(
                    wide.at[k, pl.ds(jnp.where(even, 8, halo), halo), :, cols],
                    wide.at[k, land, :, cols],
                    wp_ss.at[k, s], wp_rs.at[k, s],
                    {"gx": gx + jnp.where(even, 1, -1), "gy": gy, "gz": gz},
                )
                c.start()
                wp.append(c)
    sends += wp + wm[: 2 * nk - 2] + sp + sn

    for k in range(nk):
        sp[k].wait_recv()
        sn[k].wait_recv()
        packs = (
            jnp.where(gx == 0, 0.0, sq_p[k]),
            sq[k],
            jnp.where(gx == ngx - 1, 0.0, sq_n[k]),
        )
        for w in range(8 + 2 * halo):
            slot, x = (w - halo + 8) // 8, (w - halo) % 8
            a = pltpu.roll(packs[slot], (PADL - 8 - 8 * x) % PADL, 1)
            b = pltpu.roll(packs[slot], 64 - 8 * x, 1)
            wide[k, w, :, ny:] = jnp.where(lane < 64, b, a)
        for c in wp[2 * k : 2 * k + 2]:
            c.wait_recv()
        for c in wm[2 * k : 2 * k + 2]:
            if k < nk - 1:
                c.wait_recv()
            else:
                pl.when(has_image)(c.wait)

        @pl.when(gx == 0)
        def _():
            wide[k, 0:halo, :, :ny] = jnp.zeros((halo, 8, ny), F32)

        @pl.when(gx == ngx - 1)
        def _():
            wide[k, halo + 8 :, :, :ny] = jnp.zeros((halo, 8, ny), F32)

        if k < nk - 1:
            smooth(wide.at[k], gf)
        else:
            last[...] = wide[k]

    pl.when(low)(zl.wait_send)
    pl.when(jnp.logical_not(low))(zu.wait_send)
    for c in sends:
        c.wait_send()


def smooth(rows_ref, out_ref):
    table = cone_table()
    halo, tiles = RADIUS - 1, out_ref.shape[0]
    ny = tiles * PADL

    def row(x, carry):
        pair = [rows_ref[x + halo]]
        for a in range(1, halo + 1):
            pair.append(rows_ref[x + halo + a] + rows_ref[x + halo - a])
        total = None
        for b in range(halo + 1):
            acc = None
            for a in range(halo + 1):
                weight = float(table[RADIUS + a, RADIUS + b])
                if weight > 0.0:
                    term = weight * pair[a]
                    acc = term if acc is None else acc + term
            if b == 0:
                total = acc[:, :ny]
            else:
                total = total + (
                    pltpu.roll(acc, b, 1)[:, :ny] + pltpu.roll(acc, ny + PADL - b, 1)[:, :ny]
                )
        for t in range(tiles):
            out_ref[t, pl.ds(x, ZC, stride=8), :] = total[:, t * PADL : (t + 1) * PADL]
        return carry

    lax.fori_loop(0, 8, row, 0)


def finish(en, hn, gt, gf, last, eo, ho, gto, gfo, gl, sem):
    tiles, rows = gt.shape[0], en.shape[1]
    low = lax.axis_index("gz") == 0
    outs = []

    def store(src, dst):
        c = pltpu.make_async_copy(src, dst, sem.at[len(outs)])
        c.start()
        outs.append(c)

    n = 8 * ZC
    first = pl.multiple_of(jnp.where(low, n, 0), n)
    store(en, eo)
    for t in range(tiles):
        cols = slice(t * PADL, (t + 1) * PADL)
        store(hn.at[:, t, 8 : rows + 8, :], ho.at[:, :, cols])
        store(gt.at[t], gto.at[:, cols])
        store(gf.at[t], gfo.at[pl.ds(first, n), cols])
    smooth(last, gl)
    for t in range(tiles):
        cols = slice(t * PADL, (t + 1) * PADL)
        store(gl.at[t], gfo.at[pl.ds(n - first, n), cols])
    for c in outs:
        c.wait()


def on_device(sizes, e, h, f, material, permittivity, design_mask, grad_sum):
    nz, nx, ny = material.shape
    lay = grad_sum.shape[0]
    rows, lrows = nz * nx, lay * nx
    nchunk, nk = nz // ZC, lay // ZC
    halo, nt = RADIUS - 1, ny // PADL
    hbm = pl.BlockSpec(memory_space=pltpu.HBM)
    vmem = pl.BlockSpec(memory_space=pltpu.VMEM)
    dma = pltpu.SemaphoreType.DMA
    v = lambda *shape: pltpu.VMEM(shape, F32)
    mid = pl.pallas_call(
        functools.partial(kernel, sizes),
        out_shape=(
            v(3, rows, ny),
            v(3, nt, rows + 8, PADL),
            v(nt, lrows, PADL),
            v(nt, 8 * ZC, PADL),
            v(8 + 2 * halo, ZC, ny + PADL),
        ),
        in_specs=[
            hbm, hbm, hbm, hbm,
            hbm, hbm, hbm,
        ],
        out_specs=(vmem,) * 5,
        scratch_shapes=[
            v(3, nt, rows + 8, PADL),
            v(3, rows, ny),
            v(3, rows, ny),
            pltpu.VMEM((rows, ny), jnp.int32),
            v(lrows, ny),
            pltpu.SMEM(permittivity.shape, F32), pltpu.VMEM(design_mask.shape, jnp.int32),
            v(nchunk, 2, ZC, ny), v(nchunk, 2, ZC, ny),
            v(nchunk, 2, ZC, ny), v(nchunk, 2, ZC, ny),
            v(nchunk, 8, PADL), v(nchunk, 8, PADL),
            v(nchunk, 8, PADL), v(nchunk, 8, PADL),
            v(2, nt, 8, PADL), v(2, nt, 8, PADL),
            v(nk, 8, ZC, ny), v(nk, 8, ZC, ny),
            v(nk, 8 + 2 * halo, ZC, ny + PADL),
            v(nk, 8, PADL), v(nk, 8, PADL),
            v(nk, 8, PADL), v(nk, 8, PADL),
            v(nk, 8, PADL), v(nk, 8, PADL), v(nk, 8, PADL), v(nk, 8, PADL), v(nk, 8, PADL),
            v(halo, ZC, ny),
            dma((nt + 6,)),
            dma((nchunk,)), dma((nchunk,)), dma((nchunk,)), dma((nchunk,)),
            dma((1,)), dma((1,)), dma((nchunk,)), dma((nchunk,)),
            dma((2,)), dma((2,)),
            dma((nk, 2)), dma((nk, 2)), dma((nk, 2)), dma((nk, 2)), dma((nk, 2)), dma((nk, 2)),
            dma((nk,)), dma((nk,)), dma((nk,)), dma((nk,)),
            dma((nk,)), dma((nk,)), dma((nk,)), dma((nk,)), dma((nk,)), dma((nk,)),
        ],
        compiler_params=pltpu.CompilerParams(
            collective_id=0, has_side_effects=True, vmem_limit_bytes=63_500_000
        ),
    )(
        e.reshape(3, rows, ny), h.reshape(3, rows, ny), f.reshape(3, rows, ny),
        material.reshape(rows, ny), permittivity, design_mask, grad_sum.reshape(lrows, ny),
    )
    outs = pl.pallas_call(
        finish,
        out_shape=(
            jax.ShapeDtypeStruct((3, rows, ny), F32),
            jax.ShapeDtypeStruct((3, rows, ny), F32),
            jax.ShapeDtypeStruct((lrows, ny), F32),
            jax.ShapeDtypeStruct((lrows, ny), F32),
        ),
        in_specs=[vmem] * 5,
        out_specs=(hbm,) * 4,
        scratch_shapes=[v(nt, 8 * ZC, PADL), dma((1 + 4 * nt,))],
        compiler_params=pltpu.CompilerParams(vmem_limit_bytes=32 * 1024 * 1024),
    )(*mid)
    return (
        outs[0].reshape(3, nz, nx, ny),
        outs[1].reshape(3, nz, nx, ny),
        outs[2].reshape(lay, nx, ny),
        outs[3].reshape(lay, nx, ny),
    )


def solution(mesh):
    field = P(None, "gz", "gx", "gy")
    cells = P("gz", "gx", "gy")
    return jax.shard_map(
        functools.partial(on_device, (mesh.shape["gx"], mesh.shape["gy"])),
        mesh=mesh,
        in_specs=(field, field, field, cells, P(), P("gx", "gy"), cells),
        out_specs=(field, field, cells, cells),
        check_vma=False,
    )
```

```python
import functools

import jax
import jax.numpy as jnp
import numpy as np
from jax import lax
from jax.experimental import pallas as pl
from jax.experimental.pallas import tpu as pltpu
from jax.sharding import PartitionSpec as P

RADIUS = 6
BLOCK = 8
COURANT = 0.5
MESH = pl.DeviceIdType.MESH
F32 = jnp.float32
ZC = 8
PADL = 128


def cone_table():
    span = np.arange(2 * RADIUS + 1, dtype=np.float32) - np.float32(RADIUS)
    dist = np.sqrt(span[:, None] ** 2 + span[None, :] ** 2).astype(np.float32)
    cone = np.maximum(np.float32(RADIUS) - dist, np.float32(0.0))
    return (cone / cone.sum(dtype=np.float32)).astype(np.float32)


def kernel(
    sizes,
    e_hbm, h_hbm, f_hbm, m_hbm, perm_hbm, mask_hbm, gs_hbm,
    en, hn, gt, gf, last,
    ev, hv, fv, mv, gsv, perm_ref, mask_ref,
    xu_s, xu_r, xl_s, xl_r, yu_s, yu_r, yl_s, yl_r, zu_r, zl_r,
    xe_s, xe_r, d2_s, d2_r, d3_r, zx_r, zy_r,
    gsend, gmir, wide, el_s, er_s, el_r, er_r, turned,
    in_sem,
    xu_ss, xu_rs, xl_ss, xl_rs, yu_ss, yu_rs, yl_ss, yl_rs, z_ss, z_rs,
    m_ss, m_rs, wp_ss, wp_rs, wm_ss, wm_rs, el_ss, el_rs, er_ss, er_rs,
    d_ss, d_rs,
):
    ngx, ngy = sizes
    gx, gy, gz = lax.axis_index("gx"), lax.axis_index("gy"), lax.axis_index("gz")
    ny = fv.shape[-1]
    nchunk = m_hbm.shape[0] // (8 * ZC)
    rows = nchunk * ZC * 8
    half = ny // 2

    def dev(dx=0, dy=0):
        return {
            "gx": lax.rem(gx + (dx + ngx), ngx),
            "gy": lax.rem(gy + (dy + ngy), ngy),
            "gz": gz,
        }

    mirror = {"gx": ngx - 1 - gx, "gy": gy, "gz": gz}
    zother = {"gx": gx, "gy": gy, "gz": 1 - gz}

    even = lax.rem(gx, 2) == 0
    image_at = jnp.where(even, ngx, ngx - 2) - gx
    own_image = image_at == gx
    has_image = (gx != 0) & (gx != ngx - 1) & jnp.logical_not(own_image)
    image = {"gx": lax.rem(image_at + ngx, ngx), "gy": gy, "gz": gz}

    barrier = pltpu.get_barrier_semaphore()
    peers = [dev(dx, dy) for dx in (-1, 0, 1) for dy in (-1, 0, 1) if (dx, dy) != (0, 0)]
    peers += [mirror, zother]
    for peer in peers:
        pl.semaphore_signal(barrier, inc=1, device_id=peer, device_id_type=MESH)

    @pl.when(has_image)
    def _():
        pl.semaphore_signal(barrier, inc=1, device_id=image, device_id_type=MESH)


    def load(i, src, dst):
        c = pltpu.make_async_copy(src, dst, in_sem.at[i])
        c.start()
        return c

    tiles = ny // PADL

    def lanes(t):
        return slice(t * PADL, (t + 1) * PADL)

    def plane(ref, *at):
        lead, r = at[:-1], at[-1]
        return jnp.concatenate(
            [ref[(*lead, t, pl.ds(r, 8), slice(None))] for t in range(tiles)], 1
        )

    def put(ref, value, *at):
        lead, r = at[:-1], at[-1]
        for t in range(tiles):
            ref[(*lead, t, pl.ds(r, 8), slice(None))] = value[:, lanes(t)]

    def strided(ref, *at):
        lead, r = at[:-1], at[-1]
        return jnp.concatenate(
            [ref[(*lead, t, pl.ds(r, 8, stride=8), slice(None))] for t in range(tiles)], 1
        )

    c_e = [load(t, e_hbm.at[:, :, lanes(t)], ev.at[:, t, 0:rows, :]) for t in range(tiles)]
    c_h = [load(tiles + 5 + t, h_hbm.at[:, :, lanes(t)], hv.at[:, t]) for t in range(tiles)]
    c_m = load(tiles, m_hbm, mv)
    c_f = load(tiles + 1, f_hbm, fv)
    c_p = load(tiles + 3, perm_hbm, perm_ref)
    c_k = load(tiles + 4, mask_hbm, mask_ref)
    c_g = load(tiles + 2, gs_hbm, gsv)

    sub = lax.broadcasted_iota(jnp.int32, (8, ny), 0)
    lane = lax.broadcasted_iota(jnp.int32, (8, PADL), 1)
    zero_tile = jnp.zeros((8, PADL), F32)

    low = gz == 0
    high = jnp.logical_not(low)
    zcs = [1, jnp.where(low, 2, 0), jnp.where(low, 0, 2)]
    inner = ZC - 1

    def rows_at(z):
        return pl.multiple_of(z * 8, 8)

    def rcopy(src, dst, ss, rs, peer):
        return pltpu.make_async_remote_copy(
            src_ref=src, dst_ref=dst, send_sem=ss, recv_sem=rs, device_id=peer, device_id_type=MESH
        )

    sends = []

    def send(src, dst, sems, i, peer):
        c = rcopy(src, dst, sems[0].at[i], sems[1].at[i], peer)
        c.start()
        sends.append(c)
        return c

    for c in c_e:
        c.wait()
    ev[0:2, :, rows : rows + 8, :] = jnp.zeros((2, tiles, 8, PADL), F32)
    bottom = lax.broadcasted_iota(jnp.int32, (8, PADL), 0) == 7
    for k in range(nchunk):
        r0 = rows_at(zcs[k] * ZC)
        for i, c in enumerate((1, 2)):
            xu_s[k, i] = strided(ev, c, r0)
        d2_s[k] = ev[0, 0, pl.ds(r0 + 7, ZC, stride=8), :]
        acc = zero_tile
        for j in range(ZC):
            for i, c in enumerate((0, 2)):
                tile = ev[c, 0, pl.ds(rows_at(zcs[k] * ZC + j), 8), :]
                at = 32 * i + j
                acc = jnp.where(lane == at, pltpu.roll(tile, at, 1) if at else tile, acc)
        yu_s[k] = acc
    for t in range(tiles):
        xe_s[t : t + 1, :] = ev[2, t, 8 * inner : 8 * inner + 1, :]
    for c in c_h:
        c.wait()
    for k in range(nchunk):
        r0 = rows_at(zcs[k] * ZC)
        ex, ey, ez = (strided(ev, c, r0 + 7) for c in range(3))
        exz = strided(ev, 0, r0 + 15)
        exy = pltpu.roll(jnp.concatenate([ex, zero_tile], 1), ny + PADL - 1, 1)[:, :ny]
        xl_s[k, 0] = strided(hv, 1, r0 + 7) - COURANT * ((exz - ex) + ez)
        xl_s[k, 1] = strided(hv, 2, r0 + 7) - COURANT * ((ex - exy) - ey)
        acc = zero_tile
        for j in range(ZC):
            r = rows_at(zcs[k] * ZC + j)
            ex, ey, ez = (ev[c, tiles - 1, pl.ds(r, 8), :] for c in range(3))
            eyz = ev[1, tiles - 1, pl.ds(r + 8, 8), :]
            eyx = jnp.where(bottom, 0.0, pltpu.roll(ey, 7, 0))
            hz = hv[2, tiles - 1, pl.ds(r, 8), :] - COURANT * ((eyx - ey) + ex)
            hx = hv[0, tiles - 1, pl.ds(r, 8), :] - COURANT * ((ey - eyz) - ez)
            for i, f in enumerate((hz, hx, ey)):
                at = 32 * i + j
                acc = jnp.where(lane == at, pltpu.roll(f, at + 1, 1), acc)
        yl_s[k] = acc

    pl.semaphore_wait(barrier, len(peers) + has_image.astype(jnp.int32))
    yu = send(yu_s, yu_r, (yu_ss, yu_rs), 0, dev(0, -1))
    yl = send(yl_s, yl_r, (yl_ss, yl_rs), 0, dev(0, 1))
    xe = send(xe_s, xe_r, (d_ss, d_rs), 0, dev(-1, 0))
    d2 = send(d2_s, d2_r, (d_ss, d_rs), 1, dev(1, -1))
    d3 = send(yl_s, d3_r, (d_ss, d_rs), 2, dev(-1, 1))
    zu = rcopy(ev.at[0:2, :, 0:8, :], zu_r, z_ss.at[0], z_rs.at[0], zother)
    pl.when(high)(zu.start)
    xu, xl = [], []
    for k in range(nchunk):
        xu.append(send(xu_s.at[k], xu_r.at[k], (xu_ss, xu_rs), k, dev(-1, 0)))
        xl.append(send(xl_s.at[k], xl_r.at[k], (xl_ss, xl_rs), k, dev(1, 0)))

    c_p.wait()
    c_k.wait()
    nblk = mask_ref.shape[1]
    spread = (
        lax.broadcasted_iota(jnp.int32, (nblk, ny), 1) // BLOCK
        == lax.broadcasted_iota(jnp.int32, (nblk, ny), 0)
    ).astype(F32)
    mask = jnp.dot(
        jnp.broadcast_to(mask_ref[...].astype(F32), (8, nblk)), spread, preferred_element_type=F32
    )
    inv = [1.0 / jnp.full((8, ny), perm_ref[i], F32) for i in range(perm_ref.shape[0])]

    def shift_up_y(f, tile, at):
        tile = pltpu.roll(tile, (PADL - at) % PADL, 1) if at else tile
        return pltpu.roll(jnp.concatenate([f, tile], 1), ny + PADL - 1, 1)[:, :ny]

    def shift_up_x(f, row):
        return jnp.where(sub == 7, jnp.broadcast_to(row, (8, ny)), pltpu.roll(f, 7, 0))

    def below_inner():
        r = 8 * inner
        ex, ey, ez = (plane(ev, c, r) for c in range(3))
        exz, eyz = (plane(ev, c, r + 8) for c in range(2))
        tile = jnp.where(gy == ngy - 1, 0.0, jnp.where(low, yu_r[2], yu_r[1]))
        row = jnp.concatenate([xe_r[t : t + 1, :] for t in range(tiles)], 1)
        ezy = shift_up_y(ez, tile, 32 + inner)
        ezx = shift_up_x(ez, jnp.where(gx == ngx - 1, 0.0, row))
        put(hn, plane(hv, 0, r) - COURANT * ((ezy - ez) - (eyz - ey)), 0, r + 8)
        put(hn, plane(hv, 1, r) - COURANT * ((exz - ex) - (ezx - ez)), 1, r + 8)

    def new_h(k):
        ytile = jnp.where(gy == ngy - 1, 0.0, yu_r[k])
        xu_r[k] = jnp.where(gx == ngx - 1, 0.0, xu_r[k])
        for j in range(ZC):
            r = rows_at(zcs[k] * ZC + j)
            ex, ey, ez = (plane(ev, c, r) for c in range(3))
            exz, eyz = (plane(ev, c, r + 8) for c in range(2))
            hx, hy, hz = (plane(hv, c, r) for c in range(3))
            exy, ezy = shift_up_y(ex, ytile, j), shift_up_y(ez, ytile, 32 + j)
            eyx = shift_up_x(ey, xu_r[k, 0, j : j + 1, :])
            ezx = shift_up_x(ez, xu_r[k, 1, j : j + 1, :])
            put(hn, hx - COURANT * ((ezy - ez) - (eyz - ey)), 0, r + 8)
            put(hn, hy - COURANT * ((exz - ex) - (ezx - ez)), 1, r + 8)
            put(hn, hz - COURANT * ((eyx - ey) - (exy - ex)), 2, r + 8)

    sign = jnp.where(lane < 32, COURANT, -COURANT)
    subp = lax.broadcasted_iota(jnp.int32, (8, PADL), 0)

    def new_e(k):
        ytile = jnp.where(gy == 0, 0.0, yl_r[k])
        beside = pltpu.roll(pltpu.roll(d3_r[k], 64, 1), 7, 0)
        ytile = ytile - COURANT * jnp.where(
            (subp == 7) & (lane < 32) & (gx != ngx - 1) & (gy != 0), beside, 0.0
        )
        row_y = jnp.where(gx == 0, 0.0, xl_r[k, 0])
        row_z = jnp.where(gx == 0, 0.0, xl_r[k, 1])
        corner = jnp.where(
            (lane == PADL - 1) & (gx != 0) & (gy != ngy - 1), pltpu.roll(d2_r[k], PADL - 1, 1), 0.0
        )
        row_z = jnp.concatenate(
            [row_z[:, : ny - PADL], row_z[:, ny - PADL :] + COURANT * corner], 1
        )
        if k == 1:
            over = pltpu.roll(zy_r[...], 40, 1)
            ytile = ytile + COURANT * jnp.where((lane == 39) & low & (gy != 0), over, 0.0)
            over = jnp.concatenate([zx_r[t] for t in range(tiles)], 1)
            row_y = row_y - COURANT * jnp.where((sub == 7) & low & (gx != 0), over, 0.0)
        ytile = ytile + sign * yu_s[k]
        xl_r[k, 0] = row_y + COURANT * xu_s[k, 1]
        xl_r[k, 1] = row_z - COURANT * xu_s[k, 0]
        design = k < nchunk - 1
        l0 = zcs[k] * ZC - jnp.where(low, ZC, 0) if design else None
        for j in range(ZC):
            r = rows_at(zcs[k] * ZC + j)
            hx, hy, hz = (plane(hn, c, r + 8) for c in range(3))
            hxz, hyz = (plane(hn, c, r) for c in range(2))

            def below_y(f, at):
                tile = pltpu.roll(ytile, PADL - 1 - at, 1)
                return pltpu.roll(jnp.concatenate([f, tile], 1), 1, 1)[:, :ny]

            def below_x(f, i):
                row = jnp.broadcast_to(xl_r[k, i, j : j + 1, :], (8, ny))
                return jnp.where(sub == 0, row, pltpu.roll(f, 1, 0))

            hzy, hxy = below_y(hz, j), below_y(hx, 32 + j)
            hyx, hzx = below_x(hy, 0), below_x(hz, 1)
            m = mv[pl.ds(r, 8), :]
            gain = inv[-1]
            for i in range(len(inv) - 2, -1, -1):
                gain = jnp.where(m == i, inv[i], gain)
            gain = COURANT * gain
            curl = (
                (hz - hzy) - (hy - hyz),
                (hx - hxz) - (hz - hzx),
                (hy - hyx) - (hx - hxy),
            )
            dot = None
            for c in range(3):
                e = plane(ev, c, r) + gain * curl[c]
                en[c, pl.ds(r, 8), :] = e
                if design:
                    term = fv[c, pl.ds(r, 8), :] * e
                    dot = term if dot is None else dot + term
            if design:
                lr = rows_at(l0 + j)
                put(gt, gsv[pl.ds(lr, 8), :] + mask * dot, lr)
        return l0

    mir = []

    def send_gradient(k, l0):
        for x in range(8):
            gsend[k, x] = strided(gt, rows_at(l0) + x)
        for s in range(2):
            cols = slice(s * half, (s + 1) * half)
            mir.append(
                send(gsend.at[k, :, :, cols], gmir.at[k, :, :, cols], (m_ss.at[k], m_rs.at[k]), s, mirror)
            )

    zl = rcopy(hn.at[0:2, :, rows : rows + 8, :], zl_r, z_ss.at[1], z_rs.at[1], zother)
    zx = rcopy(zu_r.at[0], zx_r, d_ss.at[3], d_rs.at[3], dev(1, 0))
    zy = rcopy(zu_r.at[1, tiles - 1], zy_r, d_ss.at[4], d_rs.at[4], dev(0, 1))

    yu.wait_recv()
    xe.wait_recv()
    below_inner()
    xu[0].wait_recv()
    new_h(0)

    @pl.when(low)
    def _():
        zu.wait_recv()
        zx.start()
        zy.start()
        ev[0:2, :, rows : rows + 8, :] = zu_r[...]
        hn[0, :, 0:8, :] = COURANT * ev[1, :, 0:8, :]
        hn[1, :, 0:8, :] = -COURANT * ev[0, :, 0:8, :]

    xu[1].wait_recv()
    new_h(1)
    pl.when(low)(zl.start)

    c_m.wait()
    c_f.wait()
    c_g.wait()
    yl.wait_recv()
    d2.wait_recv()
    d3.wait_recv()
    xl[0].wait_recv()
    send_gradient(0, new_e(0))

    @pl.when(low)
    def _():
        zx.wait_recv()
        zy.wait_recv()

    @pl.when(high)
    def _():
        zx_r[...] = jnp.zeros((tiles, 8, PADL), F32)
        zy_r[...] = zero_tile
        zl.wait_recv()
        hn[0:2, :, 0:8, :] = zl_r[...]

    xl[1].wait_recv()
    send_gradient(1, new_e(1))

    xu[2].wait_recv()
    new_h(2)
    xl[2].wait_recv()
    new_e(2)

    halo = RADIUS - 1
    nk = nchunk - 1
    wp, wm, el, er = [], [], [], []
    for k in range(nk):
        for s in range(2):
            cols = slice(s * half, (s + 1) * half)
            mir[2 * k + s].wait_recv()
            for x in range(8):
                wide[k, halo + x, :, cols] = gsend[k, x, :, cols] + gmir[k, 7 - x, :, cols]
            acc = zero_tile
            for x in range(8):
                edge = wide[k, halo + x, :, 0:PADL] if s == 0 else wide[k, halo + x, :, ny - PADL : ny]
                at = (8 * x + 8 * s) % PADL
                acc = jnp.where((lane // 8) == x, pltpu.roll(edge, at, 1) if at else edge, acc)
            if s == 0:
                el_s[k] = acc
                for d in (0, 1, -1):
                    er.append(
                        send(el_s.at[k], er_r.at[k, 1 - d], (er_ss.at[k], er_rs.at[k]), 1 - d, dev(d, -1))
                    )
            else:
                er_s[k] = acc
                for d in (0, 1, -1):
                    el.append(
                        send(er_s.at[k], el_r.at[k, 1 - d], (el_ss.at[k], el_rs.at[k]), 1 - d, dev(d, 1))
                    )
            if k < nk - 1:
                c = rcopy(
                    wide.at[k, 8 : 8 + halo, :, cols], wide.at[k, 0:halo, :, cols],
                    wp_ss.at[k, s], wp_rs.at[k, s], dev(1, 0),
                )
                c.start()
                wp.append(c)
                c = rcopy(
                    wide.at[k, halo : 2 * halo, :, cols],
                    wide.at[k, halo + 8 : 2 * halo + 8, :, cols],
                    wm_ss.at[k, s], wm_rs.at[k, s], dev(-1, 0),
                )
                c.start()
                wm.append(c)
            else:
                for i in range(halo):
                    turned[i, :, cols] = wide[k, halo + jnp.where(even, halo - 1, 7) - i, :, cols]
                land = pl.ds(jnp.where(even, 0, halo + 8), halo)
                c = rcopy(
                    turned.at[:, :, cols], wide.at[k, land, :, cols],
                    wm_ss.at[k, s], wm_rs.at[k, s], image,
                )
                pl.when(has_image)(c.start)
                wm.append(c)

                @pl.when(own_image)
                def _():
                    wide[k, land, :, cols] = turned[:, :, cols]

                c = rcopy(
                    wide.at[k, pl.ds(jnp.where(even, 8, halo), halo), :, cols],
                    wide.at[k, land, :, cols],
                    wp_ss.at[k, s], wp_rs.at[k, s],
                    {"gx": gx + jnp.where(even, 1, -1), "gy": gy, "gz": gz},
                )
                c.start()
                wp.append(c)
    sends += wp + wm[: 2 * nk - 2]

    for k in range(nk):
        for c in el[3 * k : 3 * k + 3] + er[3 * k : 3 * k + 3]:
            c.wait_recv()
        packs = []
        for slot in range(3):
            gone = (gx == 0, gx < 0, gx == ngx - 1)[slot]
            packs.append(
                (
                    jnp.where((gy == 0) | gone, 0.0, el_r[k, slot]),
                    jnp.where((gy == ngy - 1) | gone, 0.0, er_r[k, slot]),
                )
            )
        for w in range(8 + 2 * halo):
            slot, x = (w - halo + 8) // 8, (w - halo) % 8
            a = pltpu.roll(packs[slot][0], (PADL - 8 - 8 * x) % PADL, 1)
            b = pltpu.roll(packs[slot][1], PADL - 8 * x, 1) if x else packs[slot][1]
            wide[k, w, :, ny:] = jnp.where(lane < 64, b, a)
        for c in wp[2 * k : 2 * k + 2]:
            c.wait_recv()
        for c in wm[2 * k : 2 * k + 2]:
            if k < nk - 1:
                c.wait_recv()
            else:
                pl.when(has_image)(c.wait)

        @pl.when(gx == 0)
        def _():
            wide[k, 0:halo, :, :ny] = jnp.zeros((halo, 8, ny), F32)

        @pl.when(gx == ngx - 1)
        def _():
            wide[k, halo + 8 :, :, :ny] = jnp.zeros((halo, 8, ny), F32)

        if k < nk - 1:
            smooth(wide.at[k], gf)
        else:
            last[...] = wide[k]

    @pl.when(low)
    def _():
        for c in (zl, zx, zy):
            c.wait_send()

    pl.when(high)(zu.wait_send)
    for c in sends:
        c.wait_send()


def smooth(rows_ref, out_ref):
    table = cone_table()
    halo, tiles = RADIUS - 1, out_ref.shape[0]
    ny = tiles * PADL

    def row(x, carry):
        pair = [rows_ref[x + halo]]
        for a in range(1, halo + 1):
            pair.append(rows_ref[x + halo + a] + rows_ref[x + halo - a])
        total = None
        for b in range(halo + 1):
            acc = None
            for a in range(halo + 1):
                weight = float(table[RADIUS + a, RADIUS + b])
                if weight > 0.0:
                    term = weight * pair[a]
                    acc = term if acc is None else acc + term
            if b == 0:
                total = acc[:, :ny]
            else:
                total = total + (
                    pltpu.roll(acc, b, 1)[:, :ny] + pltpu.roll(acc, ny + PADL - b, 1)[:, :ny]
                )
        for t in range(tiles):
            out_ref[t, pl.ds(x, ZC, stride=8), :] = total[:, t * PADL : (t + 1) * PADL]
        return carry

    lax.fori_loop(0, 8, row, 0)


def finish(en, hn, gt, gf, last, eo, ho, gto, gfo, gl, sem):
    tiles, rows = gt.shape[0], en.shape[1]
    low = lax.axis_index("gz") == 0
    outs = []

    def store(src, dst):
        c = pltpu.make_async_copy(src, dst, sem.at[len(outs)])
        c.start()
        outs.append(c)

    n = 8 * ZC
    first = pl.multiple_of(jnp.where(low, 0, n), n)
    store(en, eo)
    for t in range(tiles):
        cols = slice(t * PADL, (t + 1) * PADL)
        store(hn.at[:, t, 8 : rows + 8, :], ho.at[:, :, cols])
        store(gt.at[t], gto.at[:, cols])
        store(gf.at[t], gfo.at[pl.ds(first, n), cols])
    smooth(last, gl)
    for t in range(tiles):
        cols = slice(t * PADL, (t + 1) * PADL)
        store(gl.at[t], gfo.at[pl.ds(n - first, n), cols])
    for c in outs:
        c.wait()


def on_device(sizes, e, h, f, material, permittivity, design_mask, grad_sum):
    nz, nx, ny = material.shape
    lay = grad_sum.shape[0]
    rows, lrows = nz * nx, lay * nx
    nchunk, nk = nz // ZC, lay // ZC
    halo, nt = RADIUS - 1, ny // PADL
    hbm = pl.BlockSpec(memory_space=pltpu.HBM)
    vmem = pl.BlockSpec(memory_space=pltpu.VMEM)
    dma = pltpu.SemaphoreType.DMA
    v = lambda *shape: pltpu.VMEM(shape, F32)
    mid = pl.pallas_call(
        functools.partial(kernel, sizes),
        out_shape=(
            v(3, rows, ny),
            v(3, nt, rows + 8, PADL),
            v(nt, lrows, PADL),
            v(nt, 8 * ZC, PADL),
            v(8 + 2 * halo, ZC, ny + PADL),
        ),
        in_specs=[
            hbm, hbm, hbm, hbm,
            hbm, hbm, hbm,
        ],
        out_specs=(vmem,) * 5,
        scratch_shapes=[
            v(3, nt, rows + 8, PADL),
            v(3, nt, rows, PADL),
            v(3, rows, ny),
            pltpu.VMEM((rows, ny), jnp.int32),
            v(lrows, ny),
            pltpu.SMEM(permittivity.shape, F32), pltpu.VMEM(design_mask.shape, jnp.int32),
            v(nchunk, 2, ZC, ny), v(nchunk, 2, ZC, ny),
            v(nchunk, 2, ZC, ny), v(nchunk, 2, ZC, ny),
            v(nchunk, 8, PADL), v(nchunk, 8, PADL),
            v(nchunk, 8, PADL), v(nchunk, 8, PADL),
            v(2, nt, 8, PADL), v(2, nt, 8, PADL),
            v(8, PADL), v(8, PADL), v(nchunk, 8, PADL), v(nchunk, 8, PADL), v(nchunk, 8, PADL),
            v(nt, 8, PADL), v(8, PADL),
            v(nk, 8, ZC, ny), v(nk, 8, ZC, ny),
            v(nk, 8 + 2 * halo, ZC, ny + PADL),
            v(nk, 8, PADL), v(nk, 8, PADL),
            v(nk, 3, 8, PADL), v(nk, 3, 8, PADL),
            v(halo, ZC, ny),
            dma((2 * nt + 5,)),
            dma((nchunk,)), dma((nchunk,)), dma((nchunk,)), dma((nchunk,)),
            dma((1,)), dma((1,)), dma((1,)), dma((1,)),
            dma((2,)), dma((2,)),
            dma((nk, 2)), dma((nk, 2)), dma((nk, 2)), dma((nk, 2)), dma((nk, 2)), dma((nk, 2)),
            dma((nk, 3)), dma((nk, 3)), dma((nk, 3)), dma((nk, 3)),
            dma((5,)), dma((5,)),
        ],
        compiler_params=pltpu.CompilerParams(
            collective_id=0, has_side_effects=True, vmem_limit_bytes=63_500_000
        ),
    )(
        e.reshape(3, rows, ny), h.reshape(3, rows, ny), f.reshape(3, rows, ny),
        material.reshape(rows, ny), permittivity, design_mask, grad_sum.reshape(lrows, ny),
    )
    outs = pl.pallas_call(
        finish,
        out_shape=(
            jax.ShapeDtypeStruct((3, rows, ny), F32),
            jax.ShapeDtypeStruct((3, rows, ny), F32),
            jax.ShapeDtypeStruct((lrows, ny), F32),
            jax.ShapeDtypeStruct((lrows, ny), F32),
        ),
        in_specs=[vmem] * 5,
        out_specs=(hbm,) * 4,
        scratch_shapes=[v(nt, 8 * ZC, PADL), dma((1 + 4 * nt,))],
        compiler_params=pltpu.CompilerParams(vmem_limit_bytes=32 * 1024 * 1024),
    )(*mid)
    return (
        outs[0].reshape(3, nz, nx, ny),
        outs[1].reshape(3, nz, nx, ny),
        outs[2].reshape(lay, nx, ny),
        outs[3].reshape(lay, nx, ny),
    )


def solution(mesh):
    field = P(None, "gz", "gx", "gy")
    cells = P("gz", "gx", "gy")
    return jax.shard_map(
        functools.partial(on_device, (mesh.shape["gx"], mesh.shape["gy"])),
        mesh=mesh,
        in_specs=(field, field, field, cells, P(), P("gx", "gy"), cells),
        out_specs=(field, field, cells, cells),
        check_vma=False,
    )
```

```python
import functools

import jax
import jax.numpy as jnp
import numpy as np
from jax import lax
from jax.experimental import pallas as pl
from jax.experimental.pallas import tpu as pltpu
from jax.sharding import PartitionSpec as P

RADIUS = 6
BLOCK = 8
COURANT = 0.5
MESH = pl.DeviceIdType.MESH
F32 = jnp.float32
ZC = 8
PADL = 128


def cone_table():
    span = np.arange(2 * RADIUS + 1, dtype=np.float32) - np.float32(RADIUS)
    dist = np.sqrt(span[:, None] ** 2 + span[None, :] ** 2).astype(np.float32)
    cone = np.maximum(np.float32(RADIUS) - dist, np.float32(0.0))
    return (cone / cone.sum(dtype=np.float32)).astype(np.float32)


def kernel(
    sizes,
    e_hbm, h_hbm, f_hbm, m_hbm, perm_hbm, mask_hbm, gs_hbm,
    en, hn, gt, gf, last,
    ev, hv, fv, mv, gsv, perm_ref, mask_ref,
    xu_s, xu_r, xl_s, xl_r, yu_s, yu_r, yl_s, yl_r, zu_r, zl_s, zl_r,
    xe_s, xe_r, d2_s, d2_r, d3_r, zx_r, zy_r,
    gsend, gmir, wide, el_s, er_s, el_r, er_r, turned,
    in_sem,
    xu_ss, xu_rs, xl_ss, xl_rs, yu_ss, yu_rs, yl_ss, yl_rs, z_ss, z_rs,
    m_ss, m_rs, wp_ss, wp_rs, wm_ss, wm_rs, el_ss, el_rs, er_ss, er_rs,
    d_ss, d_rs,
):
    ngx, ngy = sizes
    gx, gy, gz = lax.axis_index("gx"), lax.axis_index("gy"), lax.axis_index("gz")
    ny = fv.shape[-1]
    nchunk = m_hbm.shape[0] // (8 * ZC)
    rows = nchunk * ZC * 8
    half = ny // 2

    def dev(dx=0, dy=0):
        return {
            "gx": lax.rem(gx + (dx + ngx), ngx),
            "gy": lax.rem(gy + (dy + ngy), ngy),
            "gz": gz,
        }

    mirror = {"gx": ngx - 1 - gx, "gy": gy, "gz": gz}
    zother = {"gx": gx, "gy": gy, "gz": 1 - gz}

    even = lax.rem(gx, 2) == 0
    core = lax.rem(gy, 2)
    image_at = jnp.where(even, ngx, ngx - 2) - gx
    own_image = image_at == gx
    has_image = (gx != 0) & (gx != ngx - 1) & jnp.logical_not(own_image)
    image = {"gx": lax.rem(image_at + ngx, ngx), "gy": gy, "gz": gz}

    barrier = pltpu.get_barrier_semaphore()
    peers = [dev(dx, dy) for dx in (-1, 0, 1) for dy in (-1, 0, 1) if (dx, dy) != (0, 0)]
    peers += [mirror, zother]
    for peer in peers:
        pl.semaphore_signal(barrier, inc=1, device_id=peer, device_id_type=MESH)

    @pl.when(has_image)
    def _():
        pl.semaphore_signal(barrier, inc=1, device_id=image, device_id_type=MESH)


    def load(i, src, dst):
        c = pltpu.make_async_copy(src, dst, in_sem.at[i])
        c.start()
        return c

    tiles = ny // PADL

    def lanes(t):
        return slice(t * PADL, (t + 1) * PADL)

    def plane(ref, *at):
        lead, r = at[:-1], at[-1]
        return jnp.concatenate(
            [ref[(*lead, t, pl.ds(r, 8), slice(None))] for t in range(tiles)], 1
        )

    def put(ref, value, *at):
        lead, r = at[:-1], at[-1]
        for t in range(tiles):
            ref[(*lead, t, pl.ds(r, 8), slice(None))] = value[:, lanes(t)]

    def strided(ref, *at):
        lead, r = at[:-1], at[-1]
        return jnp.concatenate(
            [ref[(*lead, t, pl.ds(r, 8, stride=8), slice(None))] for t in range(tiles)], 1
        )

    c_e = [load(t, e_hbm.at[:, :, lanes(t)], ev.at[:, t, 0:rows, :]) for t in range(tiles)]
    c_h = [load(tiles + 5 + t, h_hbm.at[:, :, lanes(t)], hv.at[:, t]) for t in range(tiles)]
    c_m = load(tiles, m_hbm, mv)
    c_f = load(tiles + 1, f_hbm, fv)
    c_p = load(tiles + 3, perm_hbm, perm_ref)
    c_k = load(tiles + 4, mask_hbm, mask_ref)
    c_g = load(tiles + 2, gs_hbm, gsv)

    sub = lax.broadcasted_iota(jnp.int32, (8, ny), 0)
    lane = lax.broadcasted_iota(jnp.int32, (8, PADL), 1)
    zero_tile = jnp.zeros((8, PADL), F32)

    low = gz == 0
    high = jnp.logical_not(low)
    zcs = [1, jnp.where(low, 2, 0), jnp.where(low, 0, 2)]
    inner = ZC - 1

    def rows_at(z):
        return pl.multiple_of(z * 8, 8)

    def rcopy(src, dst, ss, rs, peer):
        return pltpu.make_async_remote_copy(
            src_ref=src, dst_ref=dst, send_sem=ss, recv_sem=rs, device_id=peer, device_id_type=MESH
        )

    sends = []

    def send(src, dst, sems, i, peer):
        c = rcopy(src, dst, sems[0].at[i], sems[1].at[i], peer)
        c.start()
        sends.append(c)
        return c

    for c in c_e:
        c.wait()
    ev[0:2, :, rows : rows + 8, :] = jnp.zeros((2, tiles, 8, PADL), F32)
    bottom = lax.broadcasted_iota(jnp.int32, (8, PADL), 0) == 7
    for k in range(nchunk):
        r0 = rows_at(zcs[k] * ZC)
        for i, c in enumerate((1, 2)):
            xu_s[k, i] = strided(ev, c, r0)
        d2_s[k] = ev[0, 0, pl.ds(r0 + 7, ZC, stride=8), :]
        acc = zero_tile
        for j in range(ZC):
            for i, c in enumerate((0, 2)):
                tile = ev[c, 0, pl.ds(rows_at(zcs[k] * ZC + j), 8), :]
                at = 32 * i + j
                acc = jnp.where(lane == at, pltpu.roll(tile, at, 1) if at else tile, acc)
        yu_s[k] = acc
    for t in range(tiles):
        xe_s[t : t + 1, :] = ev[2, t, 8 * inner : 8 * inner + 1, :]
    pl.semaphore_wait(barrier, len(peers) + has_image.astype(jnp.int32))
    zu = rcopy(ev.at[0:2, :, 0:8, :], zu_r, z_ss.at[0], z_rs.at[0], zother)
    zl = rcopy(zl_s, zl_r, z_ss.at[1], z_rs.at[1], zother)
    pl.when(high)(zu.start)
    yu = send(yu_s, yu_r, (yu_ss, yu_rs), 0, dev(0, -1))
    xe = send(xe_s, xe_r, (d_ss, d_rs), 0, dev(-1, 0))
    d2 = send(d2_s, d2_r, (d_ss, d_rs), 1, dev(1, -1))
    xu, xl = [], []

    def send_xu(k):
        xu.append(send(xu_s.at[k], xu_r.at[k], (xu_ss, xu_rs), k, dev(-1, 0)))

    def send_xl(k):
        r0 = rows_at(zcs[k] * ZC)
        ex, ey, ez = (strided(ev, c, r0 + 7) for c in range(3))
        exz = strided(ev, 0, r0 + 15)
        exy = pltpu.roll(jnp.concatenate([ex, zero_tile], 1), ny + PADL - 1, 1)[:, :ny]
        xl_s[k, 0] = strided(hv, 1, r0 + 7) - COURANT * ((exz - ex) + ez)
        xl_s[k, 1] = strided(hv, 2, r0 + 7) - COURANT * ((ex - exy) - ey)
        xl.append(send(xl_s.at[k], xl_r.at[k], (xl_ss, xl_rs), k, dev(1, 0)))

    send_xu(0)
    for c in c_h:
        c.wait()

    @pl.when(low)
    def _():
        r = rows - 8
        ex, ey, ez = (plane(ev, c, r) for c in range(3))
        ezy = pltpu.roll(jnp.concatenate([ez, zero_tile], 1), ny + PADL - 1, 1)[:, :ny]
        ezx = jnp.where(sub == 7, 0.0, pltpu.roll(ez, 7, 0))
        put(zl_s, plane(hv, 0, r) - COURANT * ((ezy - ez) + ey), 0, 0)
        put(zl_s, plane(hv, 1, r) - COURANT * ((ez - ezx) - ex), 1, 0)
        put(zl_s, ez, 2, 0)
        zl.start()

    for k in range(nchunk):
        acc = zero_tile
        for j in range(ZC):
            r = rows_at(zcs[k] * ZC + j)
            ex, ey, ez = (ev[c, tiles - 1, pl.ds(r, 8), :] for c in range(3))
            eyz = ev[1, tiles - 1, pl.ds(r + 8, 8), :]
            eyx = jnp.where(bottom, 0.0, pltpu.roll(ey, 7, 0))
            hz = hv[2, tiles - 1, pl.ds(r, 8), :] - COURANT * ((eyx - ey) + ex)
            hx = hv[0, tiles - 1, pl.ds(r, 8), :] - COURANT * ((ey - eyz) - ez)
            for i, f in enumerate((hz, hx, ey)):
                at = 32 * i + j
                acc = jnp.where(lane == at, pltpu.roll(f, at + 1, 1), acc)
        yl_s[k] = acc
    yl = send(yl_s, yl_r, (yl_ss, yl_rs), 0, dev(0, 1))
    d3 = send(yl_s, d3_r, (d_ss, d_rs), 2, dev(-1, 1))
    send_xl(0)
    for k in range(1, nchunk):
        send_xu(k)
        send_xl(k)

    c_p.wait()
    c_k.wait()
    nblk = mask_ref.shape[1]
    spread = (
        lax.broadcasted_iota(jnp.int32, (nblk, ny), 1) // BLOCK
        == lax.broadcasted_iota(jnp.int32, (nblk, ny), 0)
    ).astype(F32)
    mask = jnp.dot(
        jnp.broadcast_to(mask_ref[...].astype(F32), (8, nblk)), spread, preferred_element_type=F32
    )
    inv = [1.0 / jnp.full((8, ny), perm_ref[i], F32) for i in range(perm_ref.shape[0])]

    def shift_up_y(f, tile, at):
        tile = pltpu.roll(tile, (PADL - at) % PADL, 1) if at else tile
        return pltpu.roll(jnp.concatenate([f, tile], 1), ny + PADL - 1, 1)[:, :ny]

    def shift_up_x(f, row):
        return jnp.where(sub == 7, jnp.broadcast_to(row, (8, ny)), pltpu.roll(f, 7, 0))

    def below_inner():
        r = 8 * inner
        ex, ey, ez = (plane(ev, c, r) for c in range(3))
        exz, eyz = (plane(ev, c, r + 8) for c in range(2))
        tile = jnp.where(gy == ngy - 1, 0.0, jnp.where(low, yu_r[2], yu_r[1]))
        row = jnp.concatenate([xe_r[t : t + 1, :] for t in range(tiles)], 1)
        ezy = shift_up_y(ez, tile, 32 + inner)
        ezx = shift_up_x(ez, jnp.where(gx == ngx - 1, 0.0, row))
        put(hn, plane(hv, 0, r) - COURANT * ((ezy - ez) - (eyz - ey)), 0, r + 8)
        put(hn, plane(hv, 1, r) - COURANT * ((exz - ex) - (ezx - ez)), 1, r + 8)

    def new_h(k):
        ytile = jnp.where(gy == ngy - 1, 0.0, yu_r[k])
        xu_r[k] = jnp.where(gx == ngx - 1, 0.0, xu_r[k])
        for j in range(ZC):
            r = rows_at(zcs[k] * ZC + j)
            ex, ey, ez = (plane(ev, c, r) for c in range(3))
            exz, eyz = (plane(ev, c, r + 8) for c in range(2))
            hx, hy, hz = (plane(hv, c, r) for c in range(3))
            exy, ezy = shift_up_y(ex, ytile, j), shift_up_y(ez, ytile, 32 + j)
            eyx = shift_up_x(ey, xu_r[k, 0, j : j + 1, :])
            ezx = shift_up_x(ez, xu_r[k, 1, j : j + 1, :])
            put(hn, hx - COURANT * ((ezy - ez) - (eyz - ey)), 0, r + 8)
            put(hn, hy - COURANT * ((exz - ex) - (ezx - ez)), 1, r + 8)
            put(hn, hz - COURANT * ((eyx - ey) - (exy - ex)), 2, r + 8)

    sign = jnp.where(lane < 32, COURANT, -COURANT)
    subp = lax.broadcasted_iota(jnp.int32, (8, PADL), 0)

    def new_e(k):
        ytile = jnp.where(gy == 0, 0.0, yl_r[k])
        beside = pltpu.roll(pltpu.roll(d3_r[k], 64, 1), 7, 0)
        ytile = ytile - COURANT * jnp.where(
            (subp == 7) & (lane < 32) & (gx != ngx - 1) & (gy != 0), beside, 0.0
        )
        row_y = jnp.where(gx == 0, 0.0, xl_r[k, 0])
        row_z = jnp.where(gx == 0, 0.0, xl_r[k, 1])
        corner = jnp.where(
            (lane == PADL - 1) & (gx != 0) & (gy != ngy - 1), pltpu.roll(d2_r[k], PADL - 1, 1), 0.0
        )
        row_z = jnp.concatenate(
            [row_z[:, : ny - PADL], row_z[:, ny - PADL :] + COURANT * corner], 1
        )
        if k == 1:
            over = pltpu.roll(zy_r[...], 40, 1)
            ytile = ytile + COURANT * jnp.where((lane == 39) & low & (gy != 0), over, 0.0)
            over = jnp.concatenate([zx_r[t] for t in range(tiles)], 1)
            row_y = row_y - COURANT * jnp.where((sub == 7) & low & (gx != 0), over, 0.0)
        ytile = ytile + sign * yu_s[k]
        xl_r[k, 0] = row_y + COURANT * xu_s[k, 1]
        xl_r[k, 1] = row_z - COURANT * xu_s[k, 0]
        design = k < nchunk - 1
        l0 = zcs[k] * ZC - jnp.where(low, ZC, 0) if design else None
        for j in range(ZC):
            r = rows_at(zcs[k] * ZC + j)
            hx, hy, hz = (plane(hn, c, r + 8) for c in range(3))
            hxz, hyz = (plane(hn, c, r) for c in range(2))

            def below_y(f, at):
                tile = pltpu.roll(ytile, PADL - 1 - at, 1)
                return pltpu.roll(jnp.concatenate([f, tile], 1), 1, 1)[:, :ny]

            def below_x(f, i):
                row = jnp.broadcast_to(xl_r[k, i, j : j + 1, :], (8, ny))
                return jnp.where(sub == 0, row, pltpu.roll(f, 1, 0))

            hzy, hxy = below_y(hz, j), below_y(hx, 32 + j)
            hyx, hzx = below_x(hy, 0), below_x(hz, 1)
            m = mv[pl.ds(r, 8), :]
            gain = inv[-1]
            for i in range(len(inv) - 2, -1, -1):
                gain = jnp.where(m == i, inv[i], gain)
            gain = COURANT * gain
            curl = (
                (hz - hzy) - (hy - hyz),
                (hx - hxz) - (hz - hzx),
                (hy - hyx) - (hx - hxy),
            )
            dot = None
            for c in range(3):
                e = plane(ev, c, r) + gain * curl[c]
                en[c, pl.ds(r, 8), :] = e
                if design:
                    term = fv[c, pl.ds(r, 8), :] * e
                    dot = term if dot is None else dot + term
            if design:
                lr = rows_at(l0 + j)
                put(gt, gsv[pl.ds(lr, 8), :] + mask * dot, lr)
        return l0

    mir = []

    def send_gradient(k, l0):
        for x in range(8):
            gsend[k, x] = strided(gt, rows_at(l0) + x)
        for s in range(2):
            cols = slice(s * half, (s + 1) * half)
            mir.append(
                send(gsend.at[k, :, :, cols], gmir.at[k, :, :, cols], (m_ss.at[k], m_rs.at[k]), s, mirror)
            )

    zx_up = rcopy(zu_r.at[0], zx_r, d_ss.at[3], d_rs.at[3], dev(1, 0))
    zy_up = rcopy(zu_r.at[1, tiles - 1], zy_r, d_ss.at[4], d_rs.at[4], dev(0, 1))
    zx_dn = rcopy(zl_r.at[2], zx_r, d_ss.at[3], d_rs.at[3], dev(-1, 0))
    zy_dn = rcopy(zl_r.at[2, 0], zy_r, d_ss.at[4], d_rs.at[4], dev(0, -1))

    yu.wait_recv()
    xe.wait_recv()
    below_inner()
    xu[0].wait_recv()
    new_h(0)

    c_m.wait()
    c_f.wait()
    c_g.wait()
    yl.wait_recv()
    d2.wait_recv()
    d3.wait_recv()
    xl[0].wait_recv()
    layer = new_e(0)

    @pl.when(low)
    def _():
        zu.wait_recv()
        zx_up.start()
        zy_up.start()
        ev[0:2, :, rows : rows + 8, :] = zu_r[...]

    @pl.when(high)
    def _():
        zl.wait_recv()
        zx_dn.start()
        zy_dn.start()

    send_gradient(0, layer)

    xu[1].wait_recv()
    new_h(1)
    xl[1].wait_recv()
    zx_up.wait_recv()
    zy_up.wait_recv()
    up_y, up_x = COURANT * ev[1, :, 0:8, :], COURANT * ev[0, :, 0:8, :]

    @pl.when(low)
    def _():
        hn[0, :, 0:8, :] = up_y
        hn[1, :, 0:8, :] = -up_x

    @pl.when(high)
    def _():
        hn[0, :, 0:8, :] = zl_r[0] + up_y
        corner = jnp.where(
            (lane == PADL - 1) & (gy != ngy - 1), pltpu.roll(zy_r[...], PADL - 1, 1), 0.0
        )
        hn[0, tiles - 1, 0:8, :] = hn[0, tiles - 1, 0:8, :] - COURANT * corner
        for t in range(tiles):
            edge = jnp.where(bottom & (gx != ngx - 1), pltpu.roll(zx_r[t], 7, 0), 0.0)
            hn[1, t, 0:8, :] = zl_r[1, t] - up_x[t] + COURANT * edge

    send_gradient(1, new_e(1))

    xu[2].wait_recv()
    new_h(2)
    xl[2].wait_recv()
    new_e(2)

    halo = RADIUS - 1
    nk = nchunk - 1
    wp, wm, el, er = [], [], [], []
    for k in range(nk):
        for s in range(2):
            cols = slice(s * half, (s + 1) * half)
            mir[2 * k + s].wait_recv()
            for x in range(8):
                wide[k, halo + x, :, cols] = gsend[k, x, :, cols] + gmir[k, 7 - x, :, cols]
            acc = zero_tile
            for x in range(8):
                edge = wide[k, halo + x, :, 0:PADL] if s == 0 else wide[k, halo + x, :, ny - PADL : ny]
                at = (8 * x + 8 * s) % PADL
                acc = jnp.where((lane // 8) == x, pltpu.roll(edge, at, 1) if at else edge, acc)
            if s == 0:
                el_s[k] = acc
                for d in (0, 1, -1):
                    rcopy(el_s.at[k], er_r.at[k, 1 - d], er_ss.at[k], er_rs.at[k], dev(d, -1)).start()
                er.append(rcopy(er_r.at[k], er_r.at[k], er_ss.at[k], er_rs.at[k], dev(0, -1)))
            else:
                er_s[k] = acc
                for d in (0, 1, -1):
                    rcopy(er_s.at[k], el_r.at[k, 1 - d], el_ss.at[k], el_rs.at[k], dev(d, 1)).start()
                el.append(rcopy(el_r.at[k], el_r.at[k], el_ss.at[k], el_rs.at[k], dev(0, 1)))
            if k < nk - 1:
                for up, ss, rs, out in ((core == 0, wp_ss, wp_rs, wp), (core == 1, wm_ss, wm_rs, wm)):
                    c = rcopy(
                        wide.at[k, pl.ds(jnp.where(up, 8, halo), halo), :, cols],
                        wide.at[k, pl.ds(jnp.where(up, 0, halo + 8), halo), :, cols],
                        ss.at[k, s], rs.at[k, s],
                        {"gx": lax.rem(gx + jnp.where(up, 1, ngx - 1), ngx), "gy": gy, "gz": gz},
                    )
                    c.start()
                    out.append(c)
            else:
                for i in range(halo):
                    turned[i, :, cols] = wide[k, halo + jnp.where(even, halo - 1, 7) - i, :, cols]
                land = pl.ds(jnp.where(even, 0, halo + 8), halo)
                c_image = rcopy(
                    turned.at[:, :, cols], wide.at[k, land, :, cols],
                    wm_ss.at[k, s], wm_rs.at[k, s], image,
                )
                pl.when(has_image & (core == 0))(c_image.start)
                c = rcopy(
                    wide.at[k, pl.ds(jnp.where(even, 8, halo), halo), :, cols],
                    wide.at[k, land, :, cols],
                    wp_ss.at[k, s], wp_rs.at[k, s],
                    {"gx": gx + jnp.where(even, 1, -1), "gy": gy, "gz": gz},
                )
                c.start()
                pl.when(has_image & (core == 1))(c_image.start)
                wp.append(c)
                wm.append(c_image)

                @pl.when(own_image)
                def _():
                    wide[k, land, :, cols] = turned[:, :, cols]

    sends += wp + wm[: 2 * nk - 2] + el + er

    for k in range(nk):
        el[k].wait_recv()
        er[k].wait_recv()
        packs = []
        for slot in range(3):
            gone = (gx == 0, gx < 0, gx == ngx - 1)[slot]
            packs.append(
                (
                    jnp.where((gy == 0) | gone, 0.0, el_r[k, slot]),
                    jnp.where((gy == ngy - 1) | gone, 0.0, er_r[k, slot]),
                )
            )
        for w in range(8 + 2 * halo):
            slot, x = (w - halo + 8) // 8, (w - halo) % 8
            a = pltpu.roll(packs[slot][0], (PADL - 8 - 8 * x) % PADL, 1)
            b = pltpu.roll(packs[slot][1], PADL - 8 * x, 1) if x else packs[slot][1]
            wide[k, w, :, ny:] = jnp.where(lane < 64, b, a)
        for c in wp[2 * k : 2 * k + 2]:
            c.wait_recv()
        for c in wm[2 * k : 2 * k + 2]:
            if k < nk - 1:
                c.wait_recv()
            else:
                pl.when(has_image)(c.wait)

        @pl.when(gx == 0)
        def _():
            wide[k, 0:halo, :, :ny] = jnp.zeros((halo, 8, ny), F32)

        @pl.when(gx == ngx - 1)
        def _():
            wide[k, halo + 8 :, :, :ny] = jnp.zeros((halo, 8, ny), F32)

        if k < nk - 1:
            smooth(wide.at[k], gf)
        else:
            last[...] = wide[k]

    zx_up.wait_send()
    zy_up.wait_send()
    pl.when(low)(zl.wait_send)
    pl.when(high)(zu.wait_send)
    for c in sends:
        c.wait_send()


def smooth(rows_ref, out_ref):
    table = cone_table()
    halo, tiles = RADIUS - 1, out_ref.shape[0]
    ny = tiles * PADL

    def row(x, carry):
        pair = [rows_ref[x + halo]]
        for a in range(1, halo + 1):
            pair.append(rows_ref[x + halo + a] + rows_ref[x + halo - a])
        total = None
        for b in range(halo + 1):
            acc = None
            for a in range(halo + 1):
                weight = float(table[RADIUS + a, RADIUS + b])
                if weight > 0.0:
                    term = weight * pair[a]
                    acc = term if acc is None else acc + term
            if b == 0:
                total = acc[:, :ny]
            else:
                total = total + (
                    pltpu.roll(acc, b, 1)[:, :ny] + pltpu.roll(acc, ny + PADL - b, 1)[:, :ny]
                )
        for t in range(tiles):
            out_ref[t, pl.ds(x, ZC, stride=8), :] = total[:, t * PADL : (t + 1) * PADL]
        return carry

    lax.fori_loop(0, 8, row, 0)


def finish(en, hn, gt, gf, last, eo, ho, gto, gfo, gl, sem):
    tiles, rows = gt.shape[0], en.shape[1]
    low = lax.axis_index("gz") == 0
    outs = []

    def store(src, dst):
        c = pltpu.make_async_copy(src, dst, sem.at[len(outs)])
        c.start()
        outs.append(c)

    n = 8 * ZC
    first = pl.multiple_of(jnp.where(low, 0, n), n)
    store(en, eo)
    for t in range(tiles):
        cols = slice(t * PADL, (t + 1) * PADL)
        store(hn.at[:, t, 8 : rows + 8, :], ho.at[:, :, cols])
        store(gt.at[t], gto.at[:, cols])
        store(gf.at[t], gfo.at[pl.ds(first, n), cols])
    smooth(last, gl)
    for t in range(tiles):
        cols = slice(t * PADL, (t + 1) * PADL)
        store(gl.at[t], gfo.at[pl.ds(n - first, n), cols])
    for c in outs:
        c.wait()


def on_device(sizes, e, h, f, material, permittivity, design_mask, grad_sum):
    nz, nx, ny = material.shape
    lay = grad_sum.shape[0]
    rows, lrows = nz * nx, lay * nx
    nchunk, nk = nz // ZC, lay // ZC
    halo, nt = RADIUS - 1, ny // PADL
    hbm = pl.BlockSpec(memory_space=pltpu.HBM)
    vmem = pl.BlockSpec(memory_space=pltpu.VMEM)
    dma = pltpu.SemaphoreType.DMA
    v = lambda *shape: pltpu.VMEM(shape, F32)
    mid = pl.pallas_call(
        functools.partial(kernel, sizes),
        out_shape=(
            v(3, rows, ny),
            v(3, nt, rows + 8, PADL),
            v(nt, lrows, PADL),
            v(nt, 8 * ZC, PADL),
            v(8 + 2 * halo, ZC, ny + PADL),
        ),
        in_specs=[
            hbm, hbm, hbm, hbm,
            hbm, hbm, hbm,
        ],
        out_specs=(vmem,) * 5,
        scratch_shapes=[
            v(3, nt, rows + 8, PADL),
            v(3, nt, rows, PADL),
            v(3, rows, ny),
            pltpu.VMEM((rows, ny), jnp.int32),
            v(lrows, ny),
            pltpu.SMEM(permittivity.shape, F32), pltpu.VMEM(design_mask.shape, jnp.int32),
            v(nchunk, 2, ZC, ny), v(nchunk, 2, ZC, ny),
            v(nchunk, 2, ZC, ny), v(nchunk, 2, ZC, ny),
            v(nchunk, 8, PADL), v(nchunk, 8, PADL),
            v(nchunk, 8, PADL), v(nchunk, 8, PADL),
            v(2, nt, 8, PADL), v(3, nt, 8, PADL), v(3, nt, 8, PADL),
            v(8, PADL), v(8, PADL), v(nchunk, 8, PADL), v(nchunk, 8, PADL), v(nchunk, 8, PADL),
            v(nt, 8, PADL), v(8, PADL),
            v(nk, 8, ZC, ny), v(nk, 8, ZC, ny),
            v(nk, 8 + 2 * halo, ZC, ny + PADL),
            v(nk, 8, PADL), v(nk, 8, PADL),
            v(nk, 3, 8, PADL), v(nk, 3, 8, PADL),
            v(halo, ZC, ny),
            dma((2 * nt + 5,)),
            dma((nchunk,)), dma((nchunk,)), dma((nchunk,)), dma((nchunk,)),
            dma((1,)), dma((1,)), dma((1,)), dma((1,)),
            dma((2,)), dma((2,)),
            dma((nk, 2)), dma((nk, 2)), dma((nk, 2)), dma((nk, 2)), dma((nk, 2)), dma((nk, 2)),
            dma((nk,)), dma((nk,)), dma((nk,)), dma((nk,)),
            dma((5,)), dma((5,)),
        ],
        compiler_params=pltpu.CompilerParams(
            collective_id=0, has_side_effects=True, vmem_limit_bytes=63_500_000
        ),
    )(
        e.reshape(3, rows, ny), h.reshape(3, rows, ny), f.reshape(3, rows, ny),
        material.reshape(rows, ny), permittivity, design_mask, grad_sum.reshape(lrows, ny),
    )
    outs = pl.pallas_call(
        finish,
        out_shape=(
            jax.ShapeDtypeStruct((3, rows, ny), F32),
            jax.ShapeDtypeStruct((3, rows, ny), F32),
            jax.ShapeDtypeStruct((lrows, ny), F32),
            jax.ShapeDtypeStruct((lrows, ny), F32),
        ),
        in_specs=[vmem] * 5,
        out_specs=(hbm,) * 4,
        scratch_shapes=[v(nt, 8 * ZC, PADL), dma((1 + 4 * nt,))],
        compiler_params=pltpu.CompilerParams(vmem_limit_bytes=32 * 1024 * 1024),
    )(*mid)
    return (
        outs[0].reshape(3, nz, nx, ny),
        outs[1].reshape(3, nz, nx, ny),
        outs[2].reshape(lay, nx, ny),
        outs[3].reshape(lay, nx, ny),
    )


def solution(mesh):
    field = P(None, "gz", "gx", "gy")
    cells = P("gz", "gx", "gy")
    return jax.shard_map(
        functools.partial(on_device, (mesh.shape["gx"], mesh.shape["gy"])),
        mesh=mesh,
        in_specs=(field, field, field, cells, P(), P("gx", "gy"), cells),
        out_specs=(field, field, cells, cells),
        check_vma=False,
    )
```
